256 devices in a mesh: ctx: 16 (over x, y_lo, core), exp: 16 (over z, y_hi).
Axes of the slice: x: 4, y: 4 (y_hi: 2, y_lo: 2; y = y_hi * 2 + y_lo), z: 8, core: 2. Of those that a mesh axis runs over, the one named last changes fastest.
Arguments:
- queries: bfloat16 [1024, 64, 512], P('ctx', 'exp'), may hold values from -17 to 17
- latent: bfloat16 [1024, 512], P('ctx'), may hold values from -2 to 2
- grad_out: bfloat16 [1024, 64, 512], P('ctx', 'exp'), may hold values from -6 to 6
- doc_ids: int32 [1024], P('ctx'), may hold values from 0 to 5, as said below
- tokens: bfloat16 [32768, 7168], P(('ctx', 'exp')), may hold values from -6 to 6
- token_grads: bfloat16 [32768, 7168], P(('ctx', 'exp')), may hold values from -1.5 to 1.5
- gate_values: float32 [32768, 8], P(('ctx', 'exp')), may hold values from 0.3 to 3
- expert_ids: int32 [32768, 8], P(('ctx', 'exp')), may hold values from 0 to 255, as said below
- gate_order: int32 [256, 128], P(('ctx', 'exp')), may hold values from 0 to 127, each once within a row
- w_gate: bfloat16 [16, 7168, 2048], P('exp', None, 'ctx'), may hold values from -0.0625 to 0.0625
- w_up: bfloat16 [16, 7168, 2048], P('exp', None, 'ctx'), may hold values from -0.0625 to 0.0625
- w_down: bfloat16 [16, 2048, 7168], P('exp', 'ctx'), may hold values from -0.125 to 0.125
Outputs:
- d_queries: bfloat16 [1024, 64, 512], P('ctx', 'exp')
- d_latent: bfloat16 [1024, 512], P('ctx')
- d_tokens: bfloat16 [32768, 7168], P(('ctx', 'exp'))
- d_gates: bfloat16 [32768, 8], P(('ctx', 'exp'))
The draws below stay inside these ranges and needn't reach their ends.
Inputs may be any that keep to these rules, and one draw needn't show every extreme that they name: `doc_ids`: never falling along the sequence; every number below 6 occurs. `expert_ids`: each row names 8 different experts. For every index of ctx some expert below 16 is named by 2 or more rows of every device at that index. `gate_order`: each row holds every number below 128 once.
All inputs are finite; a program needn't handle non-finite values.
Results may differ from the reference program's by a relative error of at most 0.02.
Values may be sent and summed in bfloat16 or wider, within the bound.
A program may use at most 128 MiB of HBM per device.

```python
import math
import jax
import jax.numpy as jnp
from jax import lax

D = 7168
HID = 2048
EXPERTS = 256
TOPK = 8
HEADS = 64
LAT = 512
SCALE_DIM = 192
T_ATT = 64
T_MOE = 128
CAP = 2
EXP_DEV = 1
DOCS = 6
N_INFL = 16
SEQ = 1024
TOKENS = 32768
N_CTX = 16
N_EXP = 16
DEVICES = 256


def latent_pairs(key):
    base_key = jax.random.fold_in(key, 7)
    first_key = jax.random.fold_in(base_key, 0)
    base_rows = jnp.clip(0.8 * jax.random.normal(first_key, (SEQ, LAT), jnp.float32), -2.0, 2.0)
    latent_rows = base_rows
    return latent_rows


def draw_latent(key, part):
    latent_rows = latent_pairs(key)
    return latent_rows.astype(jnp.bfloat16)


def draw_queries(key, part):
    own_key = jax.random.fold_in(key, 9)
    noise_key = jax.random.fold_in(own_key, 0)
    result = jnp.clip(jax.random.normal(noise_key, (SEQ, HEADS, LAT), jnp.float32), -5.0, 5.0)
    return result.astype(jnp.bfloat16)


def draw_doc_ids(key, part):
    base_key = jax.random.fold_in(key, 13)
    block_key, offset_key = jax.random.split(base_key, 2)
    chosen_blocks = jnp.sort(jax.random.permutation(block_key, N_CTX)[:DOCS - 1])
    offsets = jax.random.randint(offset_key, (DOCS - 1,), 1, T_ATT)
    bounds = (chosen_blocks * T_ATT + offsets).astype(jnp.int32)
    positions = jnp.arange(SEQ, dtype=jnp.int32)
    return jnp.sum((positions[:, None] >= bounds[None, :]).astype(jnp.int32), axis=1).astype(jnp.int32)


def draw_expert_ids(key, part):
    base_key = jax.random.fold_in(key, 11)
    noise_key, popular_key, forced_key, row_key = jax.random.split(base_key, 4)
    blocks = TOKENS // T_MOE
    jitter_values = jax.random.randint(noise_key, (TOKENS, EXPERTS), 0, 32768)
    favored_expert = jax.random.randint(popular_key, (EXPERTS,), 0, 6)
    favored_expert = favored_expert * favored_expert * 1024
    forced_expert = jax.random.randint(forced_key, (N_CTX,), 0, N_INFL)
    block_expert = jnp.repeat(forced_expert, N_EXP)
    row_scores = jax.random.randint(row_key, (blocks, T_MOE), 0, 1 << 20) * T_MOE + jnp.arange(T_MOE, dtype=jnp.int32)
    order_rank = jnp.argsort(jnp.argsort(row_scores, axis=1), axis=1)
    pinned_rows = (order_rank < CAP).reshape(TOKENS)
    expert_span = jnp.arange(EXPERTS, dtype=jnp.int32)
    row_target_expert = jnp.repeat(block_expert, T_MOE)
    favor_boost = jnp.where(pinned_rows[:, None] & (expert_span[None, :] == row_target_expert[:, None]), 1 << 30, 0)
    router_logits = (jitter_values + favored_expert[None, :]) * 256 + expert_span[None, :] + favor_boost
    ranked = jnp.argsort(-router_logits, axis=1)
    return ranked[:, :TOPK].astype(jnp.int32)


def block_scale(rng, extent, cuts, smallest, high):
    gain, own = 1.0, jax.random.fold_in(rng, 6)
    for axis_at, shards_of in cuts:
        steps = jnp.exp(jax.random.uniform(jax.random.fold_in(own, axis_at), (shards_of,), jnp.float32, smallest / len(cuts), high / len(cuts)))
        gain = gain * jnp.repeat(steps, extent[axis_at] // shards_of).reshape([-1 if axis == axis_at else 1 for axis in range(len(extent))])
    return gain


def normal_values(key, extent, deviation, reach, cuts=(), kind=jnp.bfloat16):
    drawn = jax.random.normal(key, extent, jnp.float32) * deviation
    if len(cuts) > 0:
        drawn = block_scale(key, extent, cuts, -0.22, 0.18) * drawn
    return jnp.clip(drawn, min=-reach, max=reach).astype(kind)


def setup_inputs(seed: int = 0) -> dict:
    key_list = jax.random.split(jax.random.key(seed), 13)
    queries = draw_queries(jax.random.fold_in(key_list[12], 71), 0)
    latent = draw_latent(jax.random.fold_in(key_list[12], 71), 0)
    grad_out = normal_values(key_list[2], (SEQ, HEADS, LAT), 1.0, 6.0, ((0, 16), (1, 16)))
    doc_ids = draw_doc_ids(jax.random.fold_in(key_list[12], 71), 0)
    tokens = normal_values(key_list[4], (TOKENS, D), 1.0, 6.0, ((0, 256),))
    token_grads = normal_values(key_list[5], (TOKENS, D), 0.25, 1.5, ((0, 256),))
    gate_values = jnp.clip(jnp.exp(math.log(3.0) - 2.3025851 * jax.random.uniform(key_list[6], (TOKENS, TOPK), jnp.float32) ** block_scale(key_list[6], (TOKENS, TOPK), ((0, 256),), -0.2, 0.2)), 0.3, 3.0)
    expert_ids = draw_expert_ids(jax.random.fold_in(key_list[12], 71), 0)
    gate_order = jax.vmap(lambda own: jax.random.permutation(own, T_MOE))(jax.random.split(key_list[8], DEVICES)).reshape((DEVICES, T_MOE)).astype(jnp.int32)
    w_gate = normal_values(key_list[9], (N_INFL, D, HID), D ** -0.5, 0.0625, ((0, 16), (2, 16)))
    w_up = normal_values(key_list[10], (N_INFL, D, HID), D ** -0.5, 0.0625, ((0, 16), (2, 16)))
    w_down = normal_values(key_list[11], (N_INFL, HID, D), HID ** -0.5, 0.125, ((0, 16), (1, 16)))
    return dict(queries=queries, latent=latent, grad_out=grad_out, doc_ids=doc_ids, tokens=tokens, token_grads=token_grads, gate_values=gate_values, expert_ids=expert_ids, gate_order=gate_order, w_gate=w_gate, w_up=w_up, w_down=w_down)


def attention_grads(queries, latent, grad_out, doc_ids):
    softmax_scale = SCALE_DIM ** -0.5
    allowed = doc_ids[None, :] == doc_ids[:, None]

    def one_head(carried, head_data):
        query_head, grad_head = head_data
        router_logits = softmax_scale * jnp.dot(query_head, latent.T, preferred_element_type=jnp.float32)
        router_logits = jnp.where(allowed, router_logits, -1e30)
        row_max = jnp.max(router_logits, axis=1, keepdims=True)
        unnorm = jnp.exp(router_logits - row_max)
        row_sum = jnp.sum(unnorm, axis=1, keepdims=True)
        output = jnp.dot(unnorm.astype(jnp.bfloat16), latent, preferred_element_type=jnp.float32) / row_sum
        log_sum = row_max + jnp.log(row_sum)
        delta_rows = jnp.sum(grad_head.astype(jnp.float32) * output, axis=1, keepdims=True)
        probs = jnp.exp(router_logits - log_sum)
        prob_grad = jnp.dot(grad_head, latent.T, preferred_element_type=jnp.float32)
        score_grad = (probs * (prob_grad - delta_rows)).astype(jnp.bfloat16)
        prob_weights = probs.astype(jnp.bfloat16)
        query_grad = softmax_scale * jnp.dot(score_grad, latent, preferred_element_type=jnp.float32)
        latent_grad = softmax_scale * jnp.dot(score_grad.T, query_head, preferred_element_type=jnp.float32)
        latent_grad = latent_grad + jnp.dot(prob_weights.T, grad_head, preferred_element_type=jnp.float32)
        return carried + latent_grad, query_grad.astype(jnp.bfloat16)

    heads_first = (jnp.transpose(queries, (1, 0, 2)), jnp.transpose(grad_out, (1, 0, 2)))
    latent_total, query_grads = lax.scan(one_head, jnp.zeros(latent.shape, jnp.float32), heads_first)
    return jnp.transpose(query_grads, (1, 0, 2)), latent_total.astype(jnp.bfloat16)


def expert_grads(tokens, token_grads, gate_values, expert_ids, gate_order, w_gate, w_up, w_down):
    blocks = gate_order.shape[0]
    block_rows = gate_order.shape[1]
    resident = N_EXP * EXP_DEV
    model_width = tokens.shape[1]
    shard = HID // N_CTX
    ids_blocks = expert_ids.reshape(blocks, block_rows, TOPK)
    expert_span = jnp.arange(resident, dtype=jnp.int32)
    matches = (ids_blocks[:, :, :, None] == expert_span).astype(jnp.int32)
    hits = jnp.sum(matches, axis=2)
    earlier = (gate_order[:, :, None] < gate_order[:, None, :]).astype(jnp.int32)
    ranks = jnp.einsum("but,bue->bte", earlier, hits)
    chosen = (hits[:, :, :, None] == 1) & (ranks[:, :, :, None] == jnp.arange(CAP, dtype=jnp.int32))
    chosen_int = chosen.astype(jnp.int32)
    row_index = jnp.einsum("btes,t->bes", chosen_int, jnp.arange(block_rows, dtype=jnp.int32))
    filled = jnp.sum(chosen_int, axis=1)
    block_index = jnp.arange(blocks, dtype=jnp.int32)[:, None, None]
    fill_mask = filled.astype(jnp.bfloat16)[:, :, :, None]
    picked_in = tokens.reshape(blocks, block_rows, model_width)[block_index, row_index] * fill_mask
    picked_grad = token_grads.reshape(blocks, block_rows, model_width)[block_index, row_index] * fill_mask
    rows_in = jnp.transpose(picked_in, (1, 0, 2, 3)).reshape(resident, blocks * CAP, model_width)
    rows_grad = jnp.transpose(picked_grad, (1, 0, 2, 3)).reshape(resident, blocks * CAP, model_width)

    def one_expert(expert_data):
        expert_in, expert_grad, gate_mat, up_mat, down_mat = expert_data
        gate_pre = jnp.dot(expert_in, gate_mat, preferred_element_type=jnp.float32)
        up_pre = jnp.dot(expert_in, up_mat, preferred_element_type=jnp.float32)
        act_grad = jnp.dot(expert_grad, down_mat.T, preferred_element_type=jnp.float32)
        gate_sig = jax.nn.sigmoid(gate_pre)
        silu_val = gate_pre * gate_sig
        hidden_act = (silu_val * up_pre).astype(jnp.bfloat16)
        expert_score = jnp.sum(hidden_act.astype(jnp.float32) * act_grad, axis=1)
        gate_grad = (act_grad * up_pre * gate_sig * (1.0 + gate_pre * (1.0 - gate_sig))).astype(jnp.bfloat16)
        up_grad = (act_grad * silu_val).astype(jnp.bfloat16)
        rows_total = gate_grad.shape[0]
        gate_parts = gate_grad.reshape(rows_total, N_CTX, shard).astype(jnp.float32)
        up_parts = up_grad.reshape(rows_total, N_CTX, shard).astype(jnp.float32)
        gate_tiles = gate_mat.reshape(model_width, N_CTX, shard).astype(jnp.float32)
        up_tiles = up_mat.reshape(model_width, N_CTX, shard).astype(jnp.float32)
        parts = jnp.einsum("rch,dch->rcd", gate_parts, gate_tiles, precision=lax.Precision.HIGHEST)
        parts = parts + jnp.einsum("rch,dch->rcd", up_parts, up_tiles, precision=lax.Precision.HIGHEST)
        rounded = lax.optimization_barrier(parts.astype(jnp.bfloat16))
        expert_input = jnp.sum(rounded.astype(jnp.float32), axis=1).astype(jnp.bfloat16)
        return expert_input, expert_score.astype(jnp.bfloat16)

    expert_inputs, expert_scores = lax.map(one_expert, (rows_in, rows_grad, w_gate, w_up, w_down))
    back_rows = jnp.transpose(expert_inputs.reshape(resident, blocks, CAP, model_width), (1, 0, 2, 3))
    back_scores = jnp.transpose(expert_scores.reshape(resident, blocks, CAP), (1, 0, 2))
    gate_blocks = gate_values.reshape(blocks, block_rows, TOPK)
    gate_mass = jnp.sum(matches.astype(jnp.float32) * gate_blocks[:, :, :, None], axis=2)
    weighting = chosen.astype(jnp.float32) * gate_mass[:, :, :, None]
    d_tokens = jnp.einsum("btes,besd->btd", weighting, back_rows.astype(jnp.float32), precision=lax.Precision.HIGHEST)
    kept_scores = jnp.einsum("btes,bes->bte", chosen.astype(jnp.float32), back_scores.astype(jnp.float32), precision=lax.Precision.HIGHEST)
    d_gates = jnp.einsum("btke,bte->btk", matches.astype(jnp.float32), kept_scores, precision=lax.Precision.HIGHEST)
    return d_tokens.reshape(blocks * block_rows, model_width).astype(jnp.bfloat16), d_gates.reshape(blocks * block_rows, TOPK).astype(jnp.bfloat16)


def reference(queries, latent, grad_out, doc_ids, tokens, token_grads, gate_values, expert_ids, gate_order, w_gate, w_up, w_down):
    d_queries, d_latent = attention_grads(queries, latent, grad_out, doc_ids)
    d_tokens, d_gates = expert_grads(tokens, token_grads, gate_values, expert_ids, gate_order, w_gate, w_up, w_down)
    return (d_queries, d_latent, d_tokens, d_gates)
```

```python
import functools

import jax
import jax.numpy as jnp
from jax import lax
from jax.experimental import pallas as pl
from jax.experimental.pallas import tpu as pltpu
from jax.sharding import PartitionSpec as P

SCALE = 192 ** (-0.5)
CAP = 2
MESH = pl.DeviceIdType.MESH
BF = jnp.bfloat16
F32 = jnp.float32

N_X, N_Y, N_CORE = 4, 2, 2
N_CTX, N_EXP = 16, 16
CHIPS = N_X * N_Y
D = 7168
HALF = D // 2
SHARD = 128
HID2 = 2 * SHARD
LAT = 512
KW = LAT + 128
T_ATT = 64
ROWS_ATT = 256
BLK = 64
OUTW = HALF + 128


def nt(a, b):
    return lax.dot_general(a, b, (((1,), (1,)), ((), ())), preferred_element_type=F32)


def nn(a, b):
    return lax.dot_general(a, b, (((1,), (0,)), ((), ())), preferred_element_type=F32)


def tn(a, b):
    return lax.dot_general(a, b, (((0,), (0,)), ((), ())), preferred_element_type=F32)


def kernel(
    sin_ref,
    sgr_ref,
    wg_hbm,
    wu_hbm,
    wd_hbm,
    kext_ref,
    q_ref,
    do_ref,
    qdoc_ref,
    back_ref,
    dq_ref,
    dlat_ref,
    ra,
    xg,
    wg,
    wu,
    wd,
    pbuf,
    prec,
    ggb,
    ugb,
    parts,
    rsb,
    bsend,
    kbuf,
    dsb,
    pwb,
    dkf,
    dkb,
    drec,
    s2b,
    rbuf,
    e1,
    ebuf,
    f1,
    dlat,
    sem_l,
    sem_as,
    sem_ar,
    sem_ks,
    sem_kr,
    sem_ws,
    sem_wr,
    sem_gs,
    sem_gr,
    sem_ps,
    sem_pr,
    sem_rs,
    sem_rr,
    sem_bs,
    sem_br,
    sem_ds,
    sem_dr,
):
    c = lax.axis_index("ctx")
    e = lax.axis_index("exp")
    core = lax.rem(c, 2)
    chip = lax.div(c, 2)
    y = lax.rem(chip, 2)
    x = lax.div(chip, 2)
    sib = c + 1 - 2 * core
    other = 1 - core

    def at(ctx, exp):
        return {"ctx": ctx, "exp": exp}

    def remote(src, dst, ssem, rsem, ctx, exp):
        return pltpu.make_async_remote_copy(
            src_ref=src,
            dst_ref=dst,
            send_sem=ssem,
            recv_sem=rsem,
            device_id=at(ctx, exp),
            device_id_type=MESH,
        )

    def take(ref, sem):
        pltpu.make_async_copy(ref, ref, sem).wait()

    def chip_at(r):
        return lax.rem(chip + r, CHIPS)

    lane0 = pl.multiple_of(core * SHARD, SHARD)
    own_d = pl.ds(pl.multiple_of(core * HALF, HALF), HALF)
    oth_d = pl.ds(pl.multiple_of(other * HALF, HALF), HALF)
    loc = [
        pltpu.make_async_copy(wg_hbm.at[own_d, :], wg.at[:, pl.ds(lane0, SHARD)], sem_l.at[0]),
        pltpu.make_async_copy(wu_hbm.at[own_d, :], wu.at[:, pl.ds(lane0, SHARD)], sem_l.at[1]),
        pltpu.make_async_copy(wd_hbm.at[:, own_d], wd.at[pl.ds(lane0, SHARD), :], sem_l.at[2]),
    ]
    for cp in loc:
        cp.start()

    bar = pltpu.get_barrier_semaphore()
    for r in range(CHIPS):
        for k in range(N_CORE):
            if r or k:
                to = 2 * chip_at(r) + lax.rem(core + k, 2)
                pl.semaphore_signal(bar, inc=1, device_id=at(to, e), device_id_type=MESH)
    for i in range(1, N_EXP):
        for k in range(N_CORE):
            to = 2 * chip + lax.rem(core + k, 2)
            pl.semaphore_signal(
                bar, inc=1, device_id=at(to, lax.rem(e + i, N_EXP)), device_id_type=MESH
            )
    pl.semaphore_wait(bar, 15 + 30)

    for arr, ref in enumerate((sin_ref, sgr_ref)):
        for i in range(N_EXP):
            te = lax.rem(e + i, N_EXP)
            for k in range(N_CORE):
                tc = lax.rem(core + k, 2)
                src = ref.at[te, :, pl.ds(pl.multiple_of(tc * HALF, HALF), HALF)]
                dst = ra.at[arr, core * N_EXP + e]
                if i == 0 and k == 0:
                    pltpu.make_async_copy(src, dst, sem_l.at[3 + arr]).start()
                else:
                    remote(src, dst, sem_as.at[arr], sem_ar.at[arr], 2 * chip + tc, te).start()

    for r in range(CHIPS):
        for k in range(N_CORE):
            row = (2 * ((CHIPS - r) % CHIPS) + core) * T_ATT
            dst = kbuf.at[pl.ds(pl.multiple_of(row, T_ATT), T_ATT), :]
            if r == 0 and k == 0:
                pltpu.make_async_copy(kext_ref, dst, sem_l.at[5]).start()
            else:
                to = 2 * chip_at(r) + lax.rem(core + k, 2)
                remote(kext_ref, dst, sem_ks, sem_kr, to, e).start()

    rem = [
        remote(wg_hbm.at[oth_d, :], wg.at[:, pl.ds(lane0, SHARD)], sem_ws.at[0], sem_wr.at[0], sib, e),
        remote(wu_hbm.at[oth_d, :], wu.at[:, pl.ds(lane0, SHARD)], sem_ws.at[1], sem_wr.at[1], sib, e),
        remote(wd_hbm.at[:, oth_d], wd.at[pl.ds(lane0, SHARD), :], sem_ws.at[2], sem_wr.at[2], sib, e),
    ]
    for cp in rem:
        cp.start()

    right = 4 * lax.rem(x + 1, N_X) + 2 * y + core
    left = 4 * lax.rem(x + 3, N_X) + 2 * y + core
    mate = 4 * x + 2 * (1 - y) + core

    hops = {}

    def hop(name, index, arr, dx, dy, way, lo=0, n=BLK):
        if way == "R":
            to, tx, ty = right, (dx + 3) % 4, dy
        elif way == "L":
            to, tx, ty = left, (dx + 1) % 4, dy
        else:
            to, tx, ty = mate, dx, 1 - dy
        hops[name] = remote(
            xg.at[arr, dx, pl.ds(dy * BLK + lo, n), :],
            xg.at[arr, tx, pl.ds(ty * BLK + lo, n), :],
            sem_gs.at[index],
            sem_gr.at[index],
            to,
            e,
        )
        hops[name].start()

    def got(*names):
        for name in names:
            hops[name].wait_recv()

    def repack(arr):
        pltpu.make_async_copy(
            sin_ref.at[0, :, pl.ds(0, HALF)], ra.at[arr, 0], sem_l.at[3 + arr]
        ).wait()
        take(ra.at[arr, pl.ds(0, 31)], sem_ar.at[arr])

        def body(t, carry):
            lanes = pl.ds(pl.multiple_of(t * 512, 512), 512)
            for g in range(4):
                rows = [ra[arr, 8 * g + i, :, lanes].astype(F32) for i in range(8)]
                xg[arr, 0, pl.ds(16 * g, 16), lanes] = jnp.concatenate(rows, axis=0).astype(BF)
            return carry

        lax.fori_loop(0, HALF // 512, body, 0)

    repack(0)
    hop("TY", 0, 0, 0, 0, "Y")
    hop("TR", 1, 0, 0, 0, "R")
    hop("TL", 2, 0, 0, 0, "L")
    repack(1)
    hop("GR", 3, 1, 0, 0, "R")
    hop("GL", 4, 1, 0, 0, "L")
    hop("GY", 5, 1, 0, 0, "Y")

    pltpu.make_async_copy(kext_ref, kbuf.at[pl.ds(0, T_ATT), :], sem_l.at[5]).wait()
    take(kbuf.at[pl.ds(0, 15 * T_ATT), :], sem_kr)

    def att(h, carry):
        rows = pl.ds(pl.multiple_of(h * 64, 64), 64)
        keys = kbuf[:, :LAT]
        same = nt(qdoc_ref[rows, :], kbuf[:, LAT:])
        s = nt(q_ref[rows, :], keys) * SCALE
        s = jnp.where(same > 0.5, s, -1e30)
        m = jnp.max(s, axis=1, keepdims=True)
        p = jnp.exp(s - m)
        total = jnp.sum(p, axis=1, keepdims=True)
        dp = nt(do_ref[rows, :], keys)
        delta = jnp.sum(p.astype(BF).astype(F32) * dp, axis=1, keepdims=True) / total
        probs = p / total
        ds = (probs * (dp - delta)).astype(BF)
        dsb[rows, :] = ds
        pwb[rows, :] = probs.astype(BF)
        dq_ref[rows, :] = (nn(ds, keys) * SCALE).astype(BF)
        return carry

    lax.fori_loop(0, ROWS_ATT // 64, att, 0)

    def dkeys(k, carry):
        lanes = pl.ds(pl.multiple_of(k * 128, 128), 128)
        val = tn(dsb[:, lanes], q_ref[...]) * SCALE + tn(pwb[:, lanes], do_ref[...])
        dkf[k] = val
        dkb[0, k] = val[:64].astype(BF)
        dkb[1, k] = val[64:].astype(BF)
        return carry

    lax.fori_loop(0, CHIPS, dkeys, 0)
    dk_sib = remote(dkb.at[other], drec, sem_ds.at[0], sem_dr.at[0], sib, e)
    dk_sib.start()

    got("TY")
    hop("T1R", 6, 0, 0, 1, "R")
    hop("T1L", 7, 0, 0, 1, "L")
    got("GR", "GL")
    hop("GhR", 8, 1, 3, 0, "R", 0, 32)
    hop("GhL", 9, 1, 1, 0, "L", 32, 32)
    hop("GlY", 10, 1, 3, 0, "Y")
    hop("GrY", 11, 1, 1, 0, "Y")
    got("TR", "TL")
    hop("ThR", 12, 0, 3, 0, "R", 0, 32)
    hop("ThL", 13, 0, 1, 0, "L", 32, 32)

    dk_sib.wait_recv()
    mine = pl.ds(pl.multiple_of(core * 64, 64), 64)
    dk_rs = []
    for r in range(1, CHIPS):
        s2b[r] = (dkf[r, mine, :] + drec[r].astype(F32)).astype(BF)
        cp = remote(
            s2b.at[r],
            rbuf.at[CHIPS - r - 1],
            sem_ds.at[r],
            sem_dr.at[CHIPS - r],
            2 * chip_at(r) + core,
            e,
        )
        cp.start()
        dk_rs.append(cp)

    for cp in loc:
        cp.wait()
    for cp in rem:
        cp.wait_recv()

    swaps = {}

    def forward(dx):
        xt, xd = xg[0, dx], xg[1, dx]
        pbuf[dx, 0] = nn(xt, wg[...])
        pbuf[dx, 1] = nn(xt, wu[...])
        pbuf[dx, 2] = nt(xd, wd[...])
        swaps[dx] = remote(pbuf.at[dx], prec.at[dx], sem_ps.at[dx], sem_pr.at[dx], sib, e)
        swaps[dx].start()

    owed = []

    def backward(dx):
        swaps[dx].wait_recv()
        gate = pbuf[dx, 0] + prec[dx, 0]
        up = pbuf[dx, 1] + prec[dx, 1]
        act = pbuf[dx, 2] + prec[dx, 2]
        sig = 1.0 / (1.0 + jnp.exp(-gate))
        silu = gate * sig
        hid = (silu * up).astype(BF).astype(F32)
        score = jnp.sum(hid * act, axis=1, keepdims=True)
        hi = score.astype(BF).astype(F32)
        lane = lax.broadcasted_iota(jnp.int32, (128, 128), 1)
        extra = jnp.where(lane == 0, hi, jnp.where(lane == 1, score - hi, 0.0))
        parts[dx, :, pl.ds(HALF, 128)] = extra.astype(BF)
        ggb[...] = (act * up * sig * (1.0 + gate * (1.0 - sig))).astype(BF)
        ugb[...] = (act * silu).astype(BF)

        def body(t, carry):
            cols = pl.ds(pl.multiple_of(t * 512, 512), 512)
            val = nt(ggb[...], wg[cols, :]) + nt(ugb[...], wu[cols, :])
            parts[dx, :, cols] = val.astype(BF)
            return carry

        lax.fori_loop(0, HALF // 512, body, 0)
        for dy in range(2):
            if dx or dy:
                tx = (4 - dx) % 4
                index = 2 * dx + dy
                to = 4 * lax.rem(x + dx, N_X) + 2 * lax.rem(y + dy, 2) + core
                cp = remote(
                    parts.at[dx, pl.ds(dy * BLK, BLK), :],
                    rsb.at[tx, pl.ds(dy * BLK, BLK), :],
                    sem_rs.at[index],
                    sem_rr.at[2 * tx + dy],
                    to,
                    e,
                )
                cp.start()
                owed.append((2 * tx + dy, cp))

    got("GY")
    forward(0)
    got("GhR", "GhL")
    hop("Gh0Y", 14, 1, 2, 0, "Y", 0, 32)
    hop("Gh1Y", 15, 1, 2, 0, "Y", 32, 32)
    got("T1R", "T1L")
    hop("T1hR", 16, 0, 3, 1, "R", 0, 32)
    hop("T1hL", 17, 0, 1, 1, "L", 32, 32)
    backward(0)

    for cp in dk_rs:
        cp.wait_recv()
    tot = dkf[0, mine, :] + drec[0].astype(F32)
    for r in range(CHIPS - 1):
        tot = tot + rbuf[r].astype(F32)
    e1[...] = tot.astype(BF)

    def piece(i):
        return (
            pl.ds(pl.multiple_of(lax.div(i, 4) * 16, 16), 16),
            pl.ds(pl.multiple_of(lax.rem(i, 4) * 128, 128), 128),
        )

    rows_e, lanes_e = piece(e)
    own_piece = pltpu.make_async_copy(e1.at[rows_e, lanes_e], ebuf.at[15], sem_l.at[6])
    own_piece.start()
    for i in range(1, N_EXP):
        te = lax.rem(e + i, N_EXP)
        rows_t, lanes_t = piece(te)
        remote(e1.at[rows_t, lanes_t], ebuf.at[i - 1], sem_ds.at[8], sem_dr.at[8], c, te).start()

    got("GlY")
    forward(3)
    got("GrY")
    forward(1)
    backward(3)

    own_piece.wait()
    take(ebuf.at[pl.ds(0, 15)], sem_dr.at[8])
    tot = ebuf[0].astype(F32)
    for i in range(1, N_EXP):
        tot = tot + ebuf[i].astype(F32)
    f1[...] = tot.astype(BF)
    own_final = pltpu.make_async_copy(f1, dlat.at[rows_e, lanes_e], sem_l.at[7])
    own_final.start()
    for i in range(1, N_EXP):
        te = lax.rem(e + i, N_EXP)
        remote(f1, dlat.at[rows_e, lanes_e], sem_ds.at[9], sem_dr.at[9], c, te).start()

    backward(1)
    got("ThR", "ThL", "T1hR", "T1hL", "Gh0Y", "Gh1Y")
    forward(2)
    backward(2)

    own_final.wait()
    take(ebuf.at[pl.ds(0, 15)], sem_dr.at[9])
    dlat_ref[...] = dlat[...]

    for _, cp in owed:
        cp.wait_recv()

    def total(cols):
        val = parts[0, pl.ds(0, BLK), cols].astype(F32)
        for index in range(1, 8):
            val = val + rsb[index // 2, pl.ds((index % 2) * BLK, BLK), cols].astype(F32)
        return val

    def spread(val, cols):
        for i in range(32):
            bsend[i, :, cols] = val[2 * i : 2 * i + 2, :]

    def body(t, carry):
        cols = pl.ds(pl.multiple_of(t * 256, 256), 256)
        spread(total(cols).astype(BF), cols)
        return carry

    lax.fori_loop(0, HALF // 256, body, 0)
    cols = pl.ds(HALF, 128)
    score = jnp.sum(total(cols), axis=1, keepdims=True)
    spread(jnp.broadcast_to(score, (BLK, 128)).astype(BF), cols)

    for i in range(N_EXP):
        te = lax.rem(e + i, N_EXP)
        for k in range(N_CORE):
            tc = lax.rem(core + k, 2)
            src = bsend.at[tc * N_EXP + te]
            dst = back_ref.at[core * N_EXP + e]
            if i == 0 and k == 0:
                pltpu.make_async_copy(src, dst, sem_l.at[8]).start()
            else:
                remote(src, dst, sem_bs, sem_br, 2 * chip + tc, te).start()

    take(ra.at[0, pl.ds(0, 31)], sem_as.at[0])
    take(ra.at[1, pl.ds(0, 31)], sem_as.at[1])
    take(kbuf.at[pl.ds(0, 15 * T_ATT), :], sem_ks)
    for cp in rem:
        cp.wait_send()
    for cp in hops.values():
        cp.wait_send()
    for cp in swaps.values():
        cp.wait_send()
    for _, cp in owed:
        cp.wait_send()
    dk_sib.wait_send()
    for cp in dk_rs:
        cp.wait_send()
    take(ebuf.at[pl.ds(0, 15)], sem_ds.at[8])
    take(ebuf.at[pl.ds(0, 15)], sem_ds.at[9])
    take(bsend.at[pl.ds(0, 31)], sem_bs)
    pltpu.make_async_copy(bsend.at[0], back_ref.at[0], sem_l.at[8]).wait()
    take(bsend.at[pl.ds(0, 31)], sem_br)


def fused(sin, sgr, wg, wu, wd, kext, q, do, qdoc):
    vmem = pl.BlockSpec(memory_space=pltpu.VMEM)
    hbm = pl.BlockSpec(memory_space=pl.ANY)
    dma = pltpu.SemaphoreType.DMA
    return pl.pallas_call(
        kernel,
        out_shape=(
            jax.ShapeDtypeStruct((32, 2, OUTW), BF),
            jax.ShapeDtypeStruct((ROWS_ATT, LAT), BF),
            jax.ShapeDtypeStruct((T_ATT, LAT), BF),
        ),
        in_specs=[hbm] * 5 + [vmem] * 4,
        out_specs=(vmem, vmem, vmem),
        scratch_shapes=[
            pltpu.VMEM((2, 32, 2, HALF), BF),
            pltpu.VMEM((2, N_X, 2 * BLK, HALF), BF),
            pltpu.VMEM((HALF, HID2), BF),
            pltpu.VMEM((HALF, HID2), BF),
            pltpu.VMEM((HID2, HALF), BF),
            pltpu.VMEM((N_X, 3, 2 * BLK, HID2), F32),
            pltpu.VMEM((N_X, 3, 2 * BLK, HID2), F32),
            pltpu.VMEM((2 * BLK, HID2), BF),
            pltpu.VMEM((2 * BLK, HID2), BF),
            pltpu.VMEM((N_X, 2 * BLK, OUTW), BF),
            pltpu.VMEM((N_X, 2 * BLK, OUTW), BF),
            pltpu.VMEM((32, 2, OUTW), BF),
            pltpu.VMEM((16 * T_ATT, KW), BF),
            pltpu.VMEM((ROWS_ATT, 16 * T_ATT), BF),
            pltpu.VMEM((ROWS_ATT, 16 * T_ATT), BF),
            pltpu.VMEM((CHIPS, 128, LAT), F32),
            pltpu.VMEM((2, CHIPS, 64, LAT), BF),
            pltpu.VMEM((CHIPS, 64, LAT), BF),
            pltpu.VMEM((CHIPS, 64, LAT), BF),
            pltpu.VMEM((CHIPS - 1, 64, LAT), BF),
            pltpu.VMEM((T_ATT, LAT), BF),
            pltpu.VMEM((16, 16, 128), BF),
            pltpu.VMEM((16, 128), BF),
            pltpu.VMEM((T_ATT, LAT), BF),
            dma((9,)),
            dma((2,)),
            dma((2,)),
            dma,
            dma,
            dma((3,)),
            dma((3,)),
            dma((18,)),
            dma((18,)),
            dma((4,)),
            dma((4,)),
            dma((8,)),
            dma((8,)),
            dma,
            dma,
            dma((10,)),
            dma((10,)),
        ],
        compiler_params=pltpu.CompilerParams(
            collective_id=0, has_side_effects=True, vmem_limit_bytes=60 * 1024 * 1024
        ),
        name="fused",
    )(sin, sgr, wg, wu, wd, kext, q, do, qdoc)


def local(
    queries,
    latent,
    grad_out,
    doc_ids,
    tokens,
    token_grads,
    gate_values,
    expert_ids,
    gate_order,
    w_gate,
    w_up,
    w_down,
):
    docs = jnp.arange(128, dtype=jnp.int32)
    onehot = (doc_ids[:, None] == docs).astype(BF)
    kext = jnp.concatenate([latent, onehot], axis=1)
    heads = queries.shape[1]
    qdoc = jnp.repeat(onehot, heads, axis=0)
    q = queries.reshape(ROWS_ATT, LAT)
    do = grad_out.reshape(ROWS_ATT, LAT)

    span = jnp.arange(N_EXP, dtype=jnp.int32)
    matches = (expert_ids[:, :, None] == span).astype(jnp.int32)
    hits = jnp.sum(matches, axis=1)
    priority = gate_order[0]
    earlier = (priority[:, None] < priority[None, :]).astype(jnp.int32)
    ranks = jnp.einsum("ut,ue->te", earlier, hits)
    chosen = (hits[:, :, None] == 1) & (ranks[:, :, None] == jnp.arange(CAP, dtype=jnp.int32))
    picker = chosen.astype(BF)
    sin = jnp.einsum("tes,td->esd", picker, tokens, preferred_element_type=F32).astype(BF)
    sgr = jnp.einsum("tes,td->esd", picker, token_grads, preferred_element_type=F32).astype(BF)

    back, dq, dlat = fused(
        sin, sgr, w_gate[0], w_up[0], w_down[0], kext, q, do, qdoc
    )

    rows = back.reshape(2, N_EXP, CAP, OUTW)
    gate_mass = jnp.sum(matches.astype(F32) * gate_values[:, :, None], axis=1)
    weighting = chosen.astype(F32) * gate_mass[:, :, None]
    d_tokens = jnp.einsum(
        "tes,hesd->thd",
        weighting,
        rows[..., :HALF].astype(F32),
        precision=lax.Precision.HIGHEST,
    ).reshape(tokens.shape)
    kept = jnp.einsum(
        "tes,es->te",
        chosen.astype(F32),
        rows[0, :, :, HALF].astype(F32),
        precision=lax.Precision.HIGHEST,
    )
    d_gates = jnp.einsum(
        "tke,te->tk", matches.astype(F32), kept, precision=lax.Precision.HIGHEST
    )
    return (dq.reshape(queries.shape), dlat, d_tokens.astype(BF), d_gates.astype(BF))


def solution(mesh):
    in_specs = (
        P("ctx", "exp", None),
        P("ctx", None),
        P("ctx", "exp", None),
        P("ctx"),
        P(("ctx", "exp"), None),
        P(("ctx", "exp"), None),
        P(("ctx", "exp"), None),
        P(("ctx", "exp"), None),
        P(("ctx", "exp"), None),
        P("exp", None, "ctx"),
        P("exp", None, "ctx"),
        P("exp", "ctx", None),
    )
    out_specs = (
        P("ctx", "exp", None),
        P("ctx", None),
        P(("ctx", "exp"), None),
        P(("ctx", "exp"), None),
    )
    return jax.shard_map(local, mesh=mesh, in_specs=in_specs, out_specs=out_specs, check_vma=False)
```

```python
import jax
import jax.numpy as jnp
from jax import lax
from jax.experimental import pallas as pl
from jax.experimental.pallas import tpu as pltpu
from jax.sharding import PartitionSpec as P

SCALE = 192 ** (-0.5)
MESH = pl.DeviceIdType.MESH
BF = jnp.bfloat16
F32 = jnp.float32

N_X, N_CORE = 4, 2
N_EXP = 16
CHIPS = 8
D = 7168
HALF = D // 2
SHARD = 128
HID2 = 2 * SHARD
LAT = 512
KW = LAT + 128
T_ATT = 64
ROWS_ATT = 256
BLK = 64
PAIRS = 32
EXTRA = 128
OUTW = EXTRA + HALF
STEP = 256
COLS = ((0, EXTRA + HALF // 2), (EXTRA + HALF // 2, HALF // 2))


def nt(a, b):
    return lax.dot_general(a, b, (((1,), (1,)), ((), ())), preferred_element_type=F32)


def nn(a, b):
    return lax.dot_general(a, b, (((1,), (0,)), ((), ())), preferred_element_type=F32)


def tn(a, b):
    return lax.dot_general(a, b, (((0,), (0,)), ((), ())), preferred_element_type=F32)


def route(ids, prio):
    pair = lax.broadcasted_iota(jnp.int32, (PAIRS, 128), 0)
    expert = lax.shift_right_logical(pair, 1)
    slot = (pair - 2 * expert).astype(F32)
    hits = jnp.zeros((PAIRS, 128), F32)
    for k in range(8):
        hits = hits + jnp.where(ids[k : k + 1, :] == expert, 1.0, 0.0)
    later = jnp.broadcast_to(prio.astype(F32), (128, 128))
    earlier = jnp.where(later.T < later, 1.0, 0.0)
    ranks = nn(hits.astype(BF), earlier.astype(BF))
    chosen = jnp.where((hits == 1.0) & (ranks == slot), 1.0, 0.0)
    return chosen, expert


def split_score(score):
    hi = score.astype(BF).astype(F32)
    lane = lax.broadcasted_iota(jnp.int32, (score.shape[0], EXTRA), 1)
    return jnp.where(lane == 0, hi, jnp.where(lane == 1, score - hi, 0.0)).astype(BF)


def kernel(
    ids_ref, prio_ref, docs_ref, tok_hbm, grd_hbm, wg_hbm, wu_hbm, wd_hbm, lat_hbm, q_hbm, do_hbm,
    back_ref, dq_ref, dlat_ref,
    rows_v, snd, ra, xg, wg, wu, wd, pbuf, prec, ggb, ugb, parts, rsx, rsm, s2p, rsf, rs2, ysend, rsy, bsend,
    q3, do3, qs, dos, qd, dqs, kbuf, dsb, pwb, dkf, dkb, drec, s2b, ebuf, e8, rbuf, f1, dlat,
    sem_l, sem_as, sem_ar, sem_ks, sem_kr, sem_ws, sem_wr, sem_gs, sem_gr, sem_ps, sem_pr,
    sem_rs, sem_rr, sem_bs, sem_br, sem_ds, sem_dr,
):
    c = lax.axis_index("ctx")
    e = lax.axis_index("exp")
    core = lax.rem(c, 2)
    chip = lax.div(c, 2)
    y = lax.rem(chip, 2)
    x = lax.div(chip, 2)
    sib = c + 1 - 2 * core
    other = 1 - core
    right = 4 * lax.rem(x + 1, N_X) + 2 * y + core
    left = 4 * lax.rem(x + 3, N_X) + 2 * y + core
    mate = 4 * x + 2 * (1 - y) + core

    def at(ctx, exp):
        return {"ctx": ctx, "exp": exp}

    def remote(src, dst, ssem, rsem, ctx, exp):
        return pltpu.make_async_remote_copy(
            src_ref=src,
            dst_ref=dst,
            send_sem=ssem,
            recv_sem=rsem,
            device_id=at(ctx, exp),
            device_id_type=MESH,
        )

    def take(ref, sem):
        pltpu.make_async_copy(ref, ref, sem).wait()

    def chip_at(r):
        return 2 * lax.rem(chip + r, CHIPS) + core

    lane0 = pl.multiple_of(core * SHARD, SHARD)
    own_d = pl.ds(pl.multiple_of(core * HALF, HALF), HALF)
    oth_d = pl.ds(pl.multiple_of(other * HALF, HALF), HALF)
    own_k = pl.ds(pl.multiple_of(core * 512, 512), 512)
    oth_k = pl.ds(pl.multiple_of(other * 512, 512), 512)
    own_b = pl.ds(pl.multiple_of(core * 512, 512), T_ATT)
    rows_in = [
        pltpu.make_async_copy(tok_hbm, rows_v.at[0], sem_l.at[0]),
        pltpu.make_async_copy(grd_hbm, rows_v.at[1], sem_l.at[1]),
    ]
    lat_in = pltpu.make_async_copy(lat_hbm, kbuf.at[own_b, pl.ds(0, LAT)], sem_l.at[2])
    att_in = [
        pltpu.make_async_copy(q_hbm, q3, sem_l.at[3]),
        pltpu.make_async_copy(do_hbm, do3, sem_l.at[4]),
    ]
    w_in = [
        pltpu.make_async_copy(wg_hbm.at[own_d, :], wg.at[:, pl.ds(lane0, SHARD)], sem_l.at[5]),
        pltpu.make_async_copy(wu_hbm.at[own_d, :], wu.at[:, pl.ds(lane0, SHARD)], sem_l.at[6]),
        pltpu.make_async_copy(wd_hbm.at[:, own_d], wd.at[pl.ds(lane0, SHARD), :], sem_l.at[7]),
    ]
    rows_in[0].start()
    lat_in.start()
    rows_in[1].start()

    bar = pltpu.get_barrier_semaphore()
    pl.semaphore_signal(bar, inc=1, device_id=at(sib, e), device_id_type=MESH)
    for r in range(1, CHIPS):
        pl.semaphore_signal(bar, inc=1, device_id=at(chip_at(r), e), device_id_type=MESH)
    for i in range(1, N_EXP):
        for k in range(N_CORE):
            to = at(2 * chip + lax.rem(core + k, 2), lax.rem(e + i, N_EXP))
            pl.semaphore_signal(bar, inc=1, device_id=to, device_id_type=MESH)
    for cp in att_in + w_in:
        cp.start()

    chosen, _ = route(ids_ref[...], prio_ref[...])
    picker = chosen.astype(BF)

    def pick(arr):
        rows_in[arr].wait()

        def body(t, carry):
            cols = pl.ds(pl.multiple_of(t * 512, 512), 512)
            val = nn(picker, rows_v[arr, :, cols]).astype(BF)
            snd[arr, :, :, cols] = val.reshape(N_EXP, 2, 512)
            return carry

        lax.fori_loop(0, D // 512, body, 0)

    def scatter(arr):
        for i in range(N_EXP):
            te = lax.rem(e + i, N_EXP)
            for k in range(N_CORE):
                tc = lax.rem(core + k, 2)
                src = snd.at[arr, te, :, pl.ds(pl.multiple_of(tc * HALF, HALF), HALF)]
                dst = ra.at[arr, core * N_EXP + e]
                if i == 0 and k == 0:
                    pltpu.make_async_copy(src, dst, sem_l.at[8 + arr]).start()
                else:
                    remote(src, dst, sem_as.at[arr], sem_ar.at[arr], 2 * chip + tc, te).start()

    pick(0)
    doc = lax.broadcasted_iota(jnp.int32, (128, T_ATT), 0)
    onehot_t = jnp.where(docs_ref[...] == doc, 1.0, 0.0).astype(BF)
    eye = jnp.where(
        lax.broadcasted_iota(jnp.int32, (128, 128), 0) == lax.broadcasted_iota(jnp.int32, (128, 128), 1),
        1.0,
        0.0,
    ).astype(BF)
    onehot = tn(onehot_t, eye).astype(BF)
    kbuf[own_b, pl.ds(LAT, 128)] = onehot
    lat_in.wait()

    pl.semaphore_wait(bar, 1 + 7 + 30)

    for r in range(1, CHIPS):
        row = core * 512 + (CHIPS - r) * T_ATT
        dst = kbuf.at[pl.ds(pl.multiple_of(row, T_ATT), T_ATT), :]
        remote(kbuf.at[own_b, :], dst, sem_ks.at[0], sem_kr.at[0], chip_at(r), e).start()
    scatter(0)
    pick(1)
    scatter(1)
    rem = [
        remote(wg_hbm.at[oth_d, :], wg.at[:, pl.ds(lane0, SHARD)], sem_ws.at[0], sem_wr.at[0], sib, e),
        remote(wu_hbm.at[oth_d, :], wu.at[:, pl.ds(lane0, SHARD)], sem_ws.at[1], sem_wr.at[1], sib, e),
        remote(wd_hbm.at[:, oth_d], wd.at[pl.ds(lane0, SHARD), :], sem_ws.at[2], sem_wr.at[2], sib, e),
    ]
    for cp in rem:
        cp.start()

    for cp in att_in:
        cp.wait()
    qs[...] = q3[...].reshape(ROWS_ATT, LAT)
    dos[...] = do3[...].reshape(ROWS_ATT, LAT)
    row_q = lax.shift_right_logical(lax.broadcasted_iota(jnp.int32, (ROWS_ATT, T_ATT), 0), 2)
    col_q = lax.broadcasted_iota(jnp.int32, (ROWS_ATT, T_ATT), 1)
    qd[...] = nn(jnp.where(row_q == col_q, 1.0, 0.0).astype(BF), onehot).astype(BF)

    take(kbuf.at[pl.ds(0, 7 * T_ATT), :], sem_kr.at[0])
    lat_sib = remote(kbuf.at[own_k, :], kbuf.at[own_k, :], sem_ks.at[1], sem_kr.at[1], sib, e)
    lat_sib.start()

    hops = {}

    def hop(name, index, arr, dx, dy, way, lo=0, n=BLK):
        if way == "R":
            to, tx, ty = right, (dx + 3) % 4, dy
        elif way == "L":
            to, tx, ty = left, (dx + 1) % 4, dy
        else:
            to, tx, ty = mate, dx, 1 - dy
        hops[name] = remote(
            xg.at[arr, dx, pl.ds(dy * BLK + lo, n), :],
            xg.at[arr, tx, pl.ds(ty * BLK + lo, n), :],
            sem_gs.at[index],
            sem_gr.at[index],
            to,
            e,
        )
        hops[name].start()

    def got(*names):
        for name in names:
            hops[name].wait_recv()

    def repack(arr):
        pltpu.make_async_copy(
            snd.at[0, 0, :, pl.ds(0, HALF)], ra.at[arr, 0], sem_l.at[8 + arr]
        ).wait()
        take(ra.at[arr, pl.ds(0, 31)], sem_ar.at[arr])

        def body(t, carry):
            cols = pl.ds(pl.multiple_of(t * 512, 512), 512)
            xg[arr, 0, pl.ds(0, BLK), cols] = ra[arr, :, :, cols].reshape(BLK, 512)
            return carry

        lax.fori_loop(0, HALF // 512, body, 0)

    repack(0)
    hop("TY", 0, 0, 0, 0, "Y")
    hop("TR", 1, 0, 0, 0, "R")
    hop("TL", 2, 0, 0, 0, "L")

    lat_sib.wait_recv()

    def att(h, carry):
        rows = pl.ds(pl.multiple_of(h * 64, 64), 64)
        keys = kbuf[:, :LAT]
        same = nt(qd[rows, :], kbuf[:, LAT:])
        s = nt(qs[rows, :], keys) * SCALE
        s = jnp.where(same > 0.5, s, -1e30)
        m = jnp.max(s, axis=1, keepdims=True)
        p = jnp.exp(s - m)
        total = jnp.sum(p, axis=1, keepdims=True)
        dp = nt(dos[rows, :], keys)
        delta = jnp.sum(p.astype(BF).astype(F32) * dp, axis=1, keepdims=True) / total
        probs = p / total
        ds = (probs * (dp - delta)).astype(BF)
        dsb[rows, :] = ds
        pwb[rows, :] = probs.astype(BF)
        dqs[rows, :] = (nn(ds, keys) * SCALE).astype(BF)
        return carry

    lax.fori_loop(0, ROWS_ATT // 64, att, 0)

    repack(1)
    hop("GR", 3, 1, 0, 0, "R")
    hop("GL", 4, 1, 0, 0, "L")
    hop("GY", 5, 1, 0, 0, "Y")
    got("TY")
    hop("T1R", 6, 0, 0, 1, "R")
    hop("T1L", 7, 0, 0, 1, "L")

    def dkeys(k, carry):
        rows = pl.ds(pl.multiple_of(k * 128, 128), 128)
        val = tn(dsb[:, rows], qs[...]) * SCALE + tn(pwb[:, rows], dos[...])
        dkf[rows, :] = val
        dkb[rows, :] = val.astype(BF)
        return carry

    lax.fori_loop(0, CHIPS, dkeys, 0)
    dk_sib = remote(dkb.at[oth_k, :], drec, sem_ds.at[0], sem_dr.at[0], sib, e)
    dk_sib.start()

    got("GR", "GL")
    hop("GhR", 8, 1, 3, 0, "R", 0, 32)
    hop("GhL", 9, 1, 1, 0, "L", 32, 32)
    hop("GlY", 10, 1, 3, 0, "Y")
    hop("GrY", 11, 1, 1, 0, "Y")
    got("TR", "TL")
    hop("ThR", 12, 0, 3, 0, "R", 0, 32)
    hop("ThL", 13, 0, 1, 0, "L", 32, 32)

    dk_sib.wait_recv()
    s2b[...] = (dkf[own_k, :] + drec[...].astype(F32)).astype(BF).reshape(CHIPS, T_ATT, LAT)

    def piece(i):
        return (
            pl.ds(pl.multiple_of(lax.div(i, 4) * 16, 16), 16),
            pl.ds(pl.multiple_of(lax.rem(i, 4) * 128, 128), 128),
        )

    rows_e, lanes_e = piece(e)
    own_piece = pltpu.make_async_copy(s2b.at[:, rows_e, lanes_e], ebuf.at[15], sem_l.at[10])
    own_piece.start()
    for i in range(1, N_EXP):
        te = lax.rem(e + i, N_EXP)
        rows_t, lanes_t = piece(te)
        remote(s2b.at[:, rows_t, lanes_t], ebuf.at[i - 1], sem_ds.at[8], sem_dr.at[8], c, te).start()

    for cp in w_in:
        cp.wait()
    for cp in rem:
        cp.wait_recv()

    swaps = {}

    def forward(dx):
        xt, xd = xg[0, dx], xg[1, dx]
        pbuf[dx, 0] = nn(xt, wg[...])
        pbuf[dx, 1] = nn(xt, wu[...])
        pbuf[dx, 2] = nt(xd, wd[...])
        swaps[dx] = remote(pbuf.at[dx], prec.at[dx], sem_ps.at[dx], sem_pr.at[dx], sib, e)
        swaps[dx].start()

    sends = {}

    def pass_on(kind, h, src, dst, to):
        index = 2 * kind + h
        cols = pl.ds(*COLS[h])
        sends[index] = remote(
            src.at[:, cols], dst.at[:, cols], sem_rs.at[index], sem_rr.at[index], to, e
        )
        sends[index].start()

    def passed(kind, h):
        sends[2 * kind + h].wait_recv()

    def backward(dx, done):
        swaps[dx].wait_recv()
        gate = pbuf[dx, 0] + prec[dx, 0]
        up = pbuf[dx, 1] + prec[dx, 1]
        act = pbuf[dx, 2] + prec[dx, 2]
        sig = 1.0 / (1.0 + jnp.exp(-gate))
        silu = gate * sig
        hid = (silu * up).astype(BF).astype(F32)
        parts[dx, :, pl.ds(0, EXTRA)] = split_score(jnp.sum(hid * act, axis=1, keepdims=True))
        ggb[...] = (act * up * sig * (1.0 + gate * (1.0 - sig))).astype(BF)
        ugb[...] = (act * silu).astype(BF)
        for h in range(2):

            def body(t, carry):
                at_col = h * (HALF // 2) + t * STEP
                cols = pl.ds(pl.multiple_of(at_col, STEP), STEP)
                val = nt(ggb[...], wg[cols, :]) + nt(ugb[...], wu[cols, :])
                parts[dx, :, pl.ds(pl.multiple_of(EXTRA + at_col, 128), STEP)] = val.astype(BF)
                return carry

            lax.fori_loop(0, HALF // 2 // STEP, body, 0)
            done(h)

    def merge(h, put, put_score, srcs):
        def summed(cols):
            val = srcs[0][:, cols].astype(F32)
            for ref in srcs[1:]:
                val = val + ref[:, cols].astype(F32)
            return val

        if h == 0:
            put_score(jnp.sum(summed(pl.ds(0, EXTRA)), axis=1, keepdims=True))

        def body(t, carry):
            cols = pl.ds(pl.multiple_of(EXTRA + h * (HALF // 2) + t * STEP, 128), STEP)
            put(cols, summed(cols).astype(BF))
            return carry

        lax.fori_loop(0, HALF // 2 // STEP, body, 0)

    def merge_into(h, dst, srcs):
        def put(cols, val):
            dst[:, cols] = val

        def put_score(score):
            dst[:, pl.ds(0, EXTRA)] = split_score(score)

        merge(h, put, put_score, srcs)

    mine, theirs = pl.ds(0, BLK), pl.ds(BLK, BLK)
    lo, hi = pl.ds(0, 32), pl.ds(32, 32)

    def to_right(h):
        pass_on(0, h, parts.at[1], rsx.at[0], right)

    def to_left(h):
        pass_on(1, h, parts.at[3], rsx.at[1], left)

    def to_mate(h):
        pass_on(2, h, parts.at[2, theirs], rsm, mate)

    got("GY")
    forward(0)
    got("GhR", "GhL")
    hop("Gh0Y", 14, 1, 2, 0, "Y", 0, 32)
    hop("Gh1Y", 15, 1, 2, 0, "Y", 32, 32)
    got("T1R", "T1L")
    hop("T1hR", 16, 0, 3, 1, "R", 0, 32)
    hop("T1hL", 17, 0, 1, 1, "L", 32, 32)
    got("GlY")
    forward(3)
    got("GrY")
    forward(1)
    backward(3, to_left)
    backward(1, to_right)
    backward(0, lambda h: None)

    own_piece.wait()
    take(ebuf.at[pl.ds(0, 15)], sem_dr.at[8])
    tot = ebuf[0].astype(F32)
    for i in range(1, N_EXP):
        tot = tot + ebuf[i].astype(F32)
    e8[...] = tot.astype(BF)
    for r in range(1, CHIPS):
        remote(e8.at[r], rbuf.at[CHIPS - 1 - r], sem_ds.at[1], sem_dr.at[1], chip_at(r), e).start()

    got("ThR", "ThL", "T1hR", "T1hL", "Gh0Y", "Gh1Y")
    forward(2)

    def to_mate_sum(h):
        passed(0, h)
        passed(1, h)
        merge_into(h, ysend, [parts.at[0, theirs], rsx.at[0, theirs], rsx.at[1, theirs]])
        pass_on(3, h, ysend, rsy, mate)

    to_mate_sum(0)
    backward(2, to_mate)
    for h in range(2):
        passed(2, h)
        merge_into(h, s2p, [parts.at[2, mine], rsm])
        pass_on(4, h, s2p.at[lo], rsf.at[0], right)
        pass_on(5, h, s2p.at[hi], rsf.at[1], left)
    to_mate_sum(1)
    for h in range(2):
        passed(4, h)
        pass_on(6, h, rsf.at[0], rs2.at[lo], right)
        passed(5, h)
        pass_on(7, h, rsf.at[1], rs2.at[hi], left)

    take(rbuf, sem_dr.at[1])
    tot = e8[0].astype(F32)
    for r in range(CHIPS - 1):
        tot = tot + rbuf[r].astype(F32)
    f1[...] = tot.astype(BF)
    own_final = pltpu.make_async_copy(f1, dlat.at[rows_e, lanes_e], sem_l.at[11])
    own_final.start()
    for i in range(1, N_EXP):
        te = lax.rem(e + i, N_EXP)
        remote(f1, dlat.at[rows_e, lanes_e], sem_ds.at[9], sem_dr.at[9], c, te).start()
    dq_ref[...] = dqs[...].reshape(T_ATT, 4, LAT)

    def put(cols, val):
        bsend[:, :, cols] = val.reshape(PAIRS, 2, STEP)

    def put_score(score):
        val = jnp.broadcast_to(score, (BLK, EXTRA)).astype(BF)
        bsend[:, :, pl.ds(0, EXTRA)] = val.reshape(PAIRS, 2, EXTRA)

    for h in range(2):
        passed(3, h)
        passed(6, h)
        passed(7, h)
        merge(h, put, put_score, [parts.at[0, mine], rsx.at[0, mine], rsx.at[1, mine], rsy, rs2])
        cols = pl.ds(*COLS[h])
        for i in range(N_EXP):
            te = lax.rem(e + i, N_EXP)
            for k in range(N_CORE):
                tc = lax.rem(core + k, 2)
                src = bsend.at[tc * N_EXP + te, :, cols]
                dst = back_ref.at[core * N_EXP + e, :, cols]
                if i == 0 and k == 0:
                    pltpu.make_async_copy(src, dst, sem_l.at[12 + h]).start()
                else:
                    remote(src, dst, sem_bs.at[h], sem_br.at[h], 2 * chip + tc, te).start()

    own_final.wait()
    take(ebuf.at[pl.ds(0, 15), 0], sem_dr.at[9])
    dlat_ref[...] = dlat[...]

    take(ra.at[0, pl.ds(0, 31)], sem_as.at[0])
    take(ra.at[1, pl.ds(0, 31)], sem_as.at[1])
    take(kbuf.at[pl.ds(0, 7 * T_ATT), :], sem_ks.at[0])
    lat_sib.wait_send()
    for cp in rem:
        cp.wait_send()
    for cp in hops.values():
        cp.wait_send()
    for cp in swaps.values():
        cp.wait_send()
    for cp in sends.values():
        cp.wait_send()
    dk_sib.wait_send()
    take(ebuf.at[pl.ds(0, 15)], sem_ds.at[8])
    take(rbuf, sem_ds.at[1])
    take(ebuf.at[pl.ds(0, 15), 0], sem_ds.at[9])
    for h in range(2):
        cols = pl.ds(*COLS[h])
        take(bsend.at[pl.ds(0, 31), :, cols], sem_bs.at[h])
        pltpu.make_async_copy(
            bsend.at[0, :, cols], back_ref.at[0, :, cols], sem_l.at[12 + h]
        ).wait()
        take(bsend.at[pl.ds(0, 31), :, cols], sem_br.at[h])


def fused(ids, prio, docs, tok, grd, wg, wu, wd, lat, q, do):
    vmem = pl.BlockSpec(memory_space=pltpu.VMEM)
    hbm = pl.BlockSpec(memory_space=pl.ANY)
    dma = pltpu.SemaphoreType.DMA

    def v(*shape, dtype=BF):
        return pltpu.VMEM(shape, dtype)

    return pl.pallas_call(
        kernel,
        out_shape=(
            jax.ShapeDtypeStruct((PAIRS, 2, OUTW), BF),
            jax.ShapeDtypeStruct((T_ATT, 4, LAT), BF),
            jax.ShapeDtypeStruct((T_ATT, LAT), BF),
        ),
        in_specs=[vmem] * 3 + [hbm] * 8,
        out_specs=(vmem, vmem, vmem),
        scratch_shapes=[
            v(2, 128, D),
            v(2, N_EXP, 2, D),
            v(2, PAIRS, 2, HALF),
            v(2, N_X, 2 * BLK, HALF),
            v(HALF, HID2),
            v(HALF, HID2),
            v(HID2, HALF),
            v(N_X, 3, 2 * BLK, HID2, dtype=F32),
            v(N_X, 3, 2 * BLK, HID2, dtype=F32),
            v(2 * BLK, HID2),
            v(2 * BLK, HID2),
            v(N_X, 2 * BLK, OUTW),
            v(2, 2 * BLK, OUTW),
            v(BLK, OUTW),
            v(BLK, OUTW),
            v(2, 32, OUTW),
            v(BLK, OUTW),
            v(BLK, OUTW),
            v(BLK, OUTW),
            v(PAIRS, 2, OUTW),
            v(T_ATT, 4, LAT),
            v(T_ATT, 4, LAT),
            v(ROWS_ATT, LAT),
            v(ROWS_ATT, LAT),
            v(ROWS_ATT, 128),
            v(ROWS_ATT, LAT),
            v(16 * T_ATT, KW),
            v(ROWS_ATT, 16 * T_ATT),
            v(ROWS_ATT, 16 * T_ATT),
            v(16 * T_ATT, LAT, dtype=F32),
            v(16 * T_ATT, LAT),
            v(CHIPS * T_ATT, LAT),
            v(CHIPS, T_ATT, LAT),
            v(16, CHIPS, 16, 128),
            v(CHIPS, 16, 128),
            v(CHIPS - 1, 16, 128),
            v(16, 128),
            v(T_ATT, LAT),
            dma((14,)),
            dma((2,)),
            dma((2,)),
            dma((2,)),
            dma((2,)),
            dma((3,)),
            dma((3,)),
            dma((18,)),
            dma((18,)),
            dma((4,)),
            dma((4,)),
            dma((16,)),
            dma((16,)),
            dma((2,)),
            dma((2,)),
            dma((10,)),
            dma((10,)),
        ],
        compiler_params=pltpu.CompilerParams(
            collective_id=0, has_side_effects=True, vmem_limit_bytes=58 * 1024 * 1024
        ),
        name="fused",
    )(ids, prio, docs, tok, grd, wg, wu, wd, lat, q, do)


def combine_kernel(ids_ref, prio_ref, gv_ref, back_ref, dq_in, dlat_in, dtok_ref, dg_ref, dq_ref, dlat_ref):
    ids = ids_ref[...]
    chosen, expert = route(ids, prio_ref[...])
    weight = jnp.zeros((PAIRS, 128), F32)
    for k in range(8):
        weight = weight + jnp.where(ids[k : k + 1, :] == expert, gv_ref[k : k + 1, :], 0.0)
    weight = weight * chosen
    w1 = weight.astype(BF)
    rest = weight - w1.astype(F32)
    w2 = rest.astype(BF)
    w3 = (rest - w2.astype(F32)).astype(BF)

    def body(t, carry):
        cols = pl.ds(pl.multiple_of(t * STEP, STEP), STEP)
        rows = back_ref[:, :, pl.ds(pl.multiple_of(EXTRA + t * STEP, 128), STEP)].reshape(PAIRS, STEP)
        dtok_ref[:, cols] = (tn(w3, rows) + tn(w2, rows) + tn(w1, rows)).astype(BF)
        return carry

    lax.fori_loop(0, HALF // STEP, body, 0)

    @pl.when(pl.program_id(0) == 0)
    def _():
        score = back_ref[:, :, pl.ds(0, EXTRA)].reshape(PAIRS, EXTRA).astype(F32)
        kept = chosen * score
        for k in range(8):
            own = jnp.where(ids[k : k + 1, :] == expert, kept, 0.0)
            dg_ref[k : k + 1, :] = jnp.sum(own, axis=0, keepdims=True).astype(BF)
        dq_ref[...] = dq_in[...]
        dlat_ref[...] = dlat_in[...]


def combine(ids, prio, gv, back, dq, dlat):
    def whole(shape):
        return pl.BlockSpec(shape, lambda h: (0,) * len(shape))

    return pl.pallas_call(
        combine_kernel,
        grid=(2,),
        out_shape=(
            jax.ShapeDtypeStruct((128, D), BF),
            jax.ShapeDtypeStruct((8, 128), BF),
            jax.ShapeDtypeStruct(dq.shape, BF),
            jax.ShapeDtypeStruct(dlat.shape, BF),
        ),
        in_specs=[
            whole((8, 128)),
            whole((1, 128)),
            whole((8, 128)),
            pl.BlockSpec((N_EXP, 2, OUTW), lambda h: (h, 0, 0)),
            whole(dq.shape),
            whole(dlat.shape),
        ],
        out_specs=(
            pl.BlockSpec((128, HALF), lambda h: (0, h)),
            whole((8, 128)),
            whole(dq.shape),
            whole(dlat.shape),
        ),
        name="combine",
    )(ids, prio, gv, back, dq, dlat)


def local(
    queries,
    latent,
    grad_out,
    doc_ids,
    tokens,
    token_grads,
    gate_values,
    expert_ids,
    gate_order,
    w_gate,
    w_up,
    w_down,
):
    ids = expert_ids.T
    back, dq, dlat = fused(
        ids,
        gate_order,
        doc_ids.reshape(1, T_ATT),
        tokens,
        token_grads,
        w_gate[0],
        w_up[0],
        w_down[0],
        latent,
        queries,
        grad_out,
    )
    d_tokens, d_gates, dq, dlat = combine(ids, gate_order, gate_values.T, back, dq, dlat)
    return (dq, dlat, d_tokens, d_gates.T)


def solution(mesh):
    in_specs = (
        P("ctx", "exp", None),
        P("ctx", None),
        P("ctx", "exp", None),
        P("ctx"),
        P(("ctx", "exp"), None),
        P(("ctx", "exp"), None),
        P(("ctx", "exp"), None),
        P(("ctx", "exp"), None),
        P(("ctx", "exp"), None),
        P("exp", None, "ctx"),
        P("exp", None, "ctx"),
        P("exp", "ctx", None),
    )
    out_specs = (
        P("ctx", "exp", None),
        P("ctx", None),
        P(("ctx", "exp"), None),
        P(("ctx", "exp"), None),
    )
    return jax.shard_map(local, mesh=mesh, in_specs=in_specs, out_specs=out_specs, check_vma=False)
```

```python
import jax
import jax.numpy as jnp
from jax import lax
from jax.experimental import pallas as pl
from jax.experimental.pallas import tpu as pltpu
from jax.sharding import PartitionSpec as P

SCALE = 192 ** (-0.5)
MESH = pl.DeviceIdType.MESH
BF = jnp.bfloat16
F32 = jnp.float32

N_X, N_CORE = 4, 2
N_EXP = 16
CHIPS = 8
D = 7168
HALF = D // 2
SHARD = 128
HID2 = 2 * SHARD
LAT = 512
KW = LAT + 128
T_ATT = 64
ROWS_ATT = 256
BLK = 64
PAIRS = 32
EXTRA = 128
OUTW = EXTRA + HALF
STEP = 256
HB = BLK // 2
OFFSETS = (0, 1, -1, 2, -2, 3, -3, 4, -4, 5, -5, 6, -6, 7, -7, 8)
COLS = (((0, OUTW),), ((0, EXTRA + HALF // 2), (EXTRA + HALF // 2, HALF // 2)))


def nt(a, b):
    return lax.dot_general(a, b, (((1,), (1,)), ((), ())), preferred_element_type=F32)


def nn(a, b):
    return lax.dot_general(a, b, (((1,), (0,)), ((), ())), preferred_element_type=F32)


def tn(a, b):
    return lax.dot_general(a, b, (((0,), (0,)), ((), ())), preferred_element_type=F32)


def route(ids, prio):
    pair = lax.broadcasted_iota(jnp.int32, (PAIRS, 128), 0)
    expert = lax.shift_right_logical(pair, 1)
    slot = (pair - 2 * expert).astype(F32)
    hits = jnp.zeros((PAIRS, 128), F32)
    for k in range(8):
        hits = hits + jnp.where(ids[k : k + 1, :] == expert, 1.0, 0.0)
    later = jnp.broadcast_to(prio.astype(F32), (128, 128))
    earlier = jnp.where(later.T < later, 1.0, 0.0)
    ranks = nn(hits.astype(BF), earlier.astype(BF))
    chosen = jnp.where((hits == 1.0) & (ranks == slot), 1.0, 0.0)
    return chosen, expert


def split_score(score):
    hi = score.astype(BF).astype(F32)
    lane = lax.broadcasted_iota(jnp.int32, (score.shape[0], EXTRA), 1)
    return jnp.where(lane == 0, hi, jnp.where(lane == 1, score - hi, 0.0)).astype(BF)


def kernel(
    ids_ref, prio_ref, docs_ref, tok_hbm, grd_hbm, wg_hbm, wu_hbm, wd_hbm, lat_hbm, q_hbm, do_hbm,
    back_ref, dq_ref, dlat_ref,
    rows_v, snd, ra, xg, wg, wu, wd, pbuf, prec, ggb, ugb, parts, rsx, rsm, s2p, rsf, rs2, ysend, rsy, bsend,
    q3, do3, qs, dos, qd, dqs, kbuf, dsb, pwb, dkf, dkb, drec, s2b, ebuf, e8, rbuf, f1, dlat,
    sem_l, sem_as, sem_ar, sem_ks, sem_kr, sem_ws, sem_wr, sem_gs, sem_gr, sem_ps, sem_pr,
    sem_rs, sem_rr, sem_bs, sem_br, sem_ds, sem_dr,
):
    c = lax.axis_index("ctx")
    e = lax.axis_index("exp")
    core = lax.rem(c, 2)
    chip = lax.div(c, 2)
    y = lax.rem(chip, 2)
    x = lax.div(chip, 2)
    sib = c + 1 - 2 * core
    other = 1 - core
    right = 4 * lax.rem(x + 1, N_X) + 2 * y + core
    left = 4 * lax.rem(x + 3, N_X) + 2 * y + core
    mate = 4 * x + 2 * (1 - y) + core

    def at(ctx, exp):
        return {"ctx": ctx, "exp": exp}

    def remote(src, dst, ssem, rsem, ctx, exp):
        return pltpu.make_async_remote_copy(
            src_ref=src,
            dst_ref=dst,
            send_sem=ssem,
            recv_sem=rsem,
            device_id=at(ctx, exp),
            device_id_type=MESH,
        )

    def take(ref, sem):
        pltpu.make_async_copy(ref, ref, sem).wait()

    def chip_at(r):
        return 2 * lax.rem(chip + r, CHIPS) + core

    lane0 = pl.multiple_of(core * SHARD, SHARD)
    own_d = pl.ds(pl.multiple_of(core * HALF, HALF), HALF)
    oth_d = pl.ds(pl.multiple_of(other * HALF, HALF), HALF)
    own_k = pl.ds(pl.multiple_of(core * 512, 512), 512)
    oth_k = pl.ds(pl.multiple_of(other * 512, 512), 512)
    own_b = pl.ds(pl.multiple_of(core * 512, 512), T_ATT)
    rows_in = [
        pltpu.make_async_copy(tok_hbm, rows_v.at[0], sem_l.at[0]),
        pltpu.make_async_copy(grd_hbm, rows_v.at[1], sem_l.at[1]),
    ]
    lat_in = pltpu.make_async_copy(lat_hbm, kbuf.at[own_b, pl.ds(0, LAT)], sem_l.at[2])
    att_in = [
        pltpu.make_async_copy(q_hbm, q3, sem_l.at[3]),
        pltpu.make_async_copy(do_hbm, do3, sem_l.at[4]),
    ]
    w_in = [
        pltpu.make_async_copy(wg_hbm.at[own_d, :], wg.at[:, pl.ds(lane0, SHARD)], sem_l.at[5]),
        pltpu.make_async_copy(wu_hbm.at[own_d, :], wu.at[:, pl.ds(lane0, SHARD)], sem_l.at[6]),
        pltpu.make_async_copy(wd_hbm.at[:, own_d], wd.at[pl.ds(lane0, SHARD), :], sem_l.at[7]),
    ]
    rows_in[0].start()
    lat_in.start()
    rows_in[1].start()

    bar = pltpu.get_barrier_semaphore()
    pl.semaphore_signal(bar, inc=1, device_id=at(sib, e), device_id_type=MESH)
    for r in range(1, CHIPS):
        pl.semaphore_signal(bar, inc=1, device_id=at(chip_at(r), e), device_id_type=MESH)
    for i in range(1, N_EXP):
        for k in range(N_CORE):
            to = at(2 * chip + lax.rem(core + k, 2), lax.rem(e + i, N_EXP))
            pl.semaphore_signal(bar, inc=1, device_id=to, device_id_type=MESH)
    for cp in att_in + w_in:
        cp.start()

    chosen, _ = route(ids_ref[...], prio_ref[...])
    picker = chosen.astype(BF)

    def pick(arr):
        rows_in[arr].wait()

        def body(t, carry):
            cols = pl.ds(pl.multiple_of(t * 512, 512), 512)
            val = nn(picker, rows_v[arr, :, cols]).astype(BF)
            snd[arr, :, :, cols] = val.reshape(N_EXP, 2, 512)
            return carry

        lax.fori_loop(0, D // 512, body, 0)

    def scatter(arr, b):
        for p in range(8):
            te = lax.rem(e + (N_EXP - OFFSETS[8 * b + p]) % N_EXP, N_EXP)
            for k in range(N_CORE):
                tc = lax.rem(core + k, 2)
                src = snd.at[arr, te, :, pl.ds(pl.multiple_of(tc * HALF, HALF), HALF)]
                dst = ra.at[arr, b, core * 8 + p]
                if b == 0 and p == 0 and k == 0:
                    pltpu.make_async_copy(src, dst, sem_l.at[8 + arr]).start()
                else:
                    sem = 2 * b + arr
                    remote(src, dst, sem_as.at[sem], sem_ar.at[sem], 2 * chip + tc, te).start()

    def incoming(buf, b):
        return buf.at[b, pl.ds(0, 15 + b)]

    pick(0)
    doc = lax.broadcasted_iota(jnp.int32, (128, T_ATT), 0)
    onehot_t = jnp.where(docs_ref[...] == doc, 1.0, 0.0).astype(BF)
    eye = jnp.where(
        lax.broadcasted_iota(jnp.int32, (128, 128), 0) == lax.broadcasted_iota(jnp.int32, (128, 128), 1),
        1.0,
        0.0,
    ).astype(BF)
    onehot = tn(onehot_t, eye).astype(BF)
    kbuf[own_b, pl.ds(LAT, 128)] = onehot
    lat_in.wait()

    pl.semaphore_wait(bar, 1 + 7 + 30)

    for r in range(1, CHIPS):
        row = core * 512 + (CHIPS - r) * T_ATT
        dst = kbuf.at[pl.ds(pl.multiple_of(row, T_ATT), T_ATT), :]
        remote(kbuf.at[own_b, :], dst, sem_ks.at[0], sem_kr.at[0], chip_at(r), e).start()
    scatter(0, 0)
    pick(1)
    scatter(1, 0)
    scatter(0, 1)
    scatter(1, 1)
    rem = [
        remote(wg_hbm.at[oth_d, :], wg.at[:, pl.ds(lane0, SHARD)], sem_ws.at[0], sem_wr.at[0], sib, e),
        remote(wu_hbm.at[oth_d, :], wu.at[:, pl.ds(lane0, SHARD)], sem_ws.at[1], sem_wr.at[1], sib, e),
        remote(wd_hbm.at[:, oth_d], wd.at[pl.ds(lane0, SHARD), :], sem_ws.at[2], sem_wr.at[2], sib, e),
    ]
    for cp in rem:
        cp.start()

    for cp in att_in:
        cp.wait()
    qs[...] = q3[...].reshape(ROWS_ATT, LAT)
    dos[...] = do3[...].reshape(ROWS_ATT, LAT)
    row_q = lax.shift_right_logical(lax.broadcasted_iota(jnp.int32, (ROWS_ATT, T_ATT), 0), 2)
    col_q = lax.broadcasted_iota(jnp.int32, (ROWS_ATT, T_ATT), 1)
    qd[...] = nn(jnp.where(row_q == col_q, 1.0, 0.0).astype(BF), onehot).astype(BF)

    hops = {}
    names = {}

    def hop(b, name, arr, dx, dy, way, lo=0, n=HB):
        if way == "R":
            to, tx, ty = right, (dx + 3) % 4, dy
        elif way == "L":
            to, tx, ty = left, (dx + 1) % 4, dy
        else:
            to, tx, ty = mate, dx, 1 - dy
        index = 18 * b + names.setdefault(name, len(names))
        hops[b, name] = remote(
            xg.at[arr, b, dx, pl.ds(dy * HB + lo, n), :],
            xg.at[arr, b, tx, pl.ds(ty * HB + lo, n), :],
            sem_gs.at[index],
            sem_gr.at[index],
            to,
            e,
        )
        hops[b, name].start()

    def got(b, *which):
        for name in which:
            hops[b, name].wait_recv()

    def repack(arr, b):
        if b == 0:
            pltpu.make_async_copy(
                snd.at[0, 0, :, pl.ds(0, HALF)], ra.at[arr, 0, 0], sem_l.at[8 + arr]
            ).wait()
        take(incoming(ra.at[arr], b), sem_ar.at[2 * b + arr])

        def body(t, carry):
            cols = pl.ds(pl.multiple_of(t * 512, 512), 512)
            xg[arr, b, 0, pl.ds(0, HB), cols] = ra[arr, b, :, :, cols].reshape(HB, 512)
            return carry

        lax.fori_loop(0, HALF // 512, body, 0)

    def hops_own(b):
        repack(0, b)
        hop(b, "TY", 0, 0, 0, "Y")
        hop(b, "TR", 0, 0, 0, "R")
        hop(b, "TL", 0, 0, 0, "L")
        repack(1, b)
        hop(b, "GR", 1, 0, 0, "R")
        hop(b, "GL", 1, 0, 0, "L")
        hop(b, "GY", 1, 0, 0, "Y")

    def hops_second(b):
        got(b, "TY")
        hop(b, "T1R", 0, 0, 1, "R")
        hop(b, "T1L", 0, 0, 1, "L")
        got(b, "GR", "GL")
        hop(b, "GlY", 1, 3, 0, "Y")
        hop(b, "GrY", 1, 1, 0, "Y")
        hop(b, "GhR", 1, 3, 0, "R", 0, HB // 2)
        hop(b, "GhL", 1, 1, 0, "L", HB // 2, HB // 2)
        got(b, "TR", "TL")
        hop(b, "ThR", 0, 3, 0, "R", 0, HB // 2)
        hop(b, "ThL", 0, 1, 0, "L", HB // 2, HB // 2)

    def hops_third(b):
        got(b, "GhR", "GhL")
        hop(b, "Gh0Y", 1, 2, 0, "Y", 0, HB // 2)
        hop(b, "Gh1Y", 1, 2, 0, "Y", HB // 2, HB // 2)
        got(b, "T1R", "T1L")
        hop(b, "T1hR", 0, 3, 1, "R", 0, HB // 2)
        hop(b, "T1hL", 0, 1, 1, "L", HB // 2, HB // 2)

    hops_own(0)
    take(kbuf.at[pl.ds(0, 7 * T_ATT), :], sem_kr.at[0])
    lat_sib = remote(kbuf.at[own_k, :], kbuf.at[own_k, :], sem_ks.at[1], sem_kr.at[1], sib, e)
    lat_sib.start()

    lat_sib.wait_recv()

    def att(h, carry):
        rows = pl.ds(pl.multiple_of(h * 64, 64), 64)
        keys = kbuf[:, :LAT]
        same = nt(qd[rows, :], kbuf[:, LAT:])
        s = nt(qs[rows, :], keys) * SCALE
        s = jnp.where(same > 0.5, s, -1e30)
        m = jnp.max(s, axis=1, keepdims=True)
        p = jnp.exp(s - m)
        total = jnp.sum(p, axis=1, keepdims=True)
        dp = nt(dos[rows, :], keys)
        delta = jnp.sum(p.astype(BF).astype(F32) * dp, axis=1, keepdims=True) / total
        probs = p / total
        ds = (probs * (dp - delta)).astype(BF)
        dsb[rows, :] = ds
        pwb[rows, :] = probs.astype(BF)
        dqs[rows, :] = (nn(ds, keys) * SCALE).astype(BF)
        return carry

    lax.fori_loop(0, ROWS_ATT // 64, att, 0)

    hops_second(0)

    def dkeys(k, carry):
        rows = pl.ds(pl.multiple_of(k * 128, 128), 128)
        val = tn(dsb[:, rows], qs[...]) * SCALE + tn(pwb[:, rows], dos[...])
        dkf[rows, :] = val
        dkb[rows, :] = val.astype(BF)
        return carry

    lax.fori_loop(0, CHIPS, dkeys, 0)
    dk_sib = remote(dkb.at[oth_k, :], drec, sem_ds.at[0], sem_dr.at[0], sib, e)
    dk_sib.start()

    for cp in w_in:
        cp.wait()
    for cp in rem:
        cp.wait_recv()

    swaps = {}

    def forward(b, dx):
        xt, xd = xg[0, b, dx], xg[1, b, dx]
        pbuf[b, dx, 0] = nn(xt, wg[...])
        pbuf[b, dx, 1] = nn(xt, wu[...])
        pbuf[b, dx, 2] = nt(xd, wd[...])
        index = 4 * b + dx
        swaps[b, dx] = remote(
            pbuf.at[b, dx], prec.at[b, dx], sem_ps.at[index], sem_pr.at[index], sib, e
        )
        swaps[b, dx].start()

    sends = {}

    def pass_on(kind, b, h, src, dst, to):
        index = 3 * kind + b + h
        cols = pl.ds(*COLS[b][h])
        sends[kind, b, h] = remote(
            src.at[:, cols], dst.at[:, cols], sem_rs.at[index], sem_rr.at[index], to, e
        )
        sends[kind, b, h].start()

    def passed(kind, b, h):
        sends[kind, b, h].wait_recv()

    def wide(b, h):
        start, n = COLS[b][h]
        first = max(start - EXTRA, 0)
        return first, (start + n - EXTRA - first) // STEP

    def backward(b, dx, done):
        swaps[b, dx].wait_recv()
        gate = pbuf[b, dx, 0] + prec[b, dx, 0]
        up = pbuf[b, dx, 1] + prec[b, dx, 1]
        act = pbuf[b, dx, 2] + prec[b, dx, 2]
        sig = 1.0 / (1.0 + jnp.exp(-gate))
        silu = gate * sig
        hid = (silu * up).astype(BF).astype(F32)
        parts[b, dx, :, pl.ds(0, EXTRA)] = split_score(jnp.sum(hid * act, axis=1, keepdims=True))
        ggb[...] = (act * up * sig * (1.0 + gate * (1.0 - sig))).astype(BF)
        ugb[...] = (act * silu).astype(BF)
        for h in range(len(COLS[b])):
            first, steps = wide(b, h)

            def body(t, carry):
                at_col = first + t * STEP
                cols = pl.ds(pl.multiple_of(at_col, STEP), STEP)
                val = nt(ggb[...], wg[cols, :]) + nt(ugb[...], wu[cols, :])
                parts[b, dx, :, pl.ds(pl.multiple_of(EXTRA + at_col, 128), STEP)] = val.astype(BF)
                return carry

            lax.fori_loop(0, steps, body, 0)
            if done is not None:
                done(b, h)

    def merge(b, h, put, put_score, srcs):
        def summed(cols):
            val = srcs[0][:, cols].astype(F32)
            for ref in srcs[1:]:
                val = val + ref[:, cols].astype(F32)
            return val

        if h == 0:
            put_score(jnp.sum(summed(pl.ds(0, EXTRA)), axis=1, keepdims=True))
        first, steps = wide(b, h)

        def body(t, carry):
            cols = pl.ds(pl.multiple_of(EXTRA + first + t * STEP, 128), STEP)
            put(cols, summed(cols).astype(BF))
            return carry

        lax.fori_loop(0, steps, body, 0)

    def merge_into(b, h, dst, srcs):
        def put(cols, val):
            dst[:, cols] = val

        def put_score(score):
            dst[:, pl.ds(0, EXTRA)] = split_score(score)

        merge(b, h, put, put_score, srcs)

    mine, theirs = pl.ds(0, HB), pl.ds(HB, HB)
    lo, hi = pl.ds(0, HB // 2), pl.ds(HB // 2, HB // 2)

    def to_right(b, h):
        pass_on(0, b, h, parts.at[b, 1], rsx.at[b, 0], right)

    def to_left(b, h):
        pass_on(1, b, h, parts.at[b, 3], rsx.at[b, 1], left)

    def to_mate(b, h):
        pass_on(2, b, h, parts.at[b, 2, theirs], rsm.at[b], mate)

    def to_mate_sum(b, h):
        passed(0, b, h)
        passed(1, b, h)
        merge_into(
            b, h, ysend.at[b], [parts.at[b, 0, theirs], rsx.at[b, 0, theirs], rsx.at[b, 1, theirs]]
        )
        pass_on(3, b, h, ysend.at[b], rsy.at[b], mate)

    def to_far(b, h):
        passed(2, b, h)
        merge_into(b, h, s2p.at[b], [parts.at[b, 2, mine], rsm.at[b]])
        pass_on(4, b, h, s2p.at[b, lo], rsf.at[b, 0], right)
        pass_on(5, b, h, s2p.at[b, hi], rsf.at[b, 1], left)

    def to_far_again(b, h):
        passed(4, b, h)
        pass_on(6, b, h, rsf.at[b, 0], rs2.at[b, lo], right)
        passed(5, b, h)
        pass_on(7, b, h, rsf.at[b, 1], rs2.at[b, hi], left)

    def give_back(b, h):
        def put(cols, val):
            bsend[b, :, :, cols] = val.reshape(16, 2, STEP)

        def put_score(score):
            val = jnp.broadcast_to(score, (HB, EXTRA)).astype(BF)
            bsend[b, :, :, pl.ds(0, EXTRA)] = val.reshape(16, 2, EXTRA)

        passed(3, b, h)
        passed(6, b, h)
        passed(7, b, h)
        merge(
            b,
            h,
            put,
            put_score,
            [parts.at[b, 0, mine], rsx.at[b, 0, mine], rsx.at[b, 1, mine], rsy.at[b], rs2.at[b]],
        )
        cols = pl.ds(*COLS[b][h])
        for p in range(8):
            te = lax.rem(e + OFFSETS[8 * b + p] % N_EXP, N_EXP)
            for k in range(N_CORE):
                tc = lax.rem(core + k, 2)
                src = bsend.at[b, tc * 8 + p, :, cols]
                dst = back_ref.at[core * N_EXP + e, :, cols]
                if b == 0 and p == 0 and k == 0:
                    pltpu.make_async_copy(src, dst, sem_l.at[12]).start()
                else:
                    remote(
                        src, dst, sem_bs.at[b + h], sem_br.at[b + h], 2 * chip + tc, te
                    ).start()

    got(0, "GY")
    forward(0, 0)
    hops_own(1)
    hops_third(0)

    dk_sib.wait_recv()
    s2b[...] = (dkf[own_k, :] + drec[...].astype(F32)).astype(BF).reshape(CHIPS, T_ATT, LAT)

    def piece(i):
        return (
            pl.ds(pl.multiple_of(lax.div(i, 4) * 16, 16), 16),
            pl.ds(pl.multiple_of(lax.rem(i, 4) * 128, 128), 128),
        )

    rows_e, lanes_e = piece(e)
    own_piece = pltpu.make_async_copy(s2b.at[:, rows_e, lanes_e], ebuf.at[15], sem_l.at[10])
    own_piece.start()
    for i in range(1, N_EXP):
        te = lax.rem(e + i, N_EXP)
        rows_t, lanes_t = piece(te)
        remote(s2b.at[:, rows_t, lanes_t], ebuf.at[i - 1], sem_ds.at[8], sem_dr.at[8], c, te).start()

    got(0, "GlY")
    forward(0, 3)
    got(0, "GrY")
    forward(0, 1)
    backward(0, 3, to_left)
    backward(0, 1, to_right)
    hops_second(1)
    got(0, "ThR", "ThL", "T1hR", "T1hL", "Gh0Y", "Gh1Y")
    forward(0, 2)
    backward(0, 0, None)
    backward(0, 2, to_mate)
    got(1, "GY")
    forward(1, 0)
    hops_third(1)
    to_mate_sum(0, 0)
    to_far(0, 0)
    got(1, "GlY")
    forward(1, 3)
    got(1, "GrY")
    forward(1, 1)
    backward(1, 3, to_left)
    backward(1, 1, to_right)
    to_far_again(0, 0)

    own_piece.wait()
    take(ebuf.at[pl.ds(0, 15)], sem_dr.at[8])
    tot = ebuf[0].astype(F32)
    for i in range(1, N_EXP):
        tot = tot + ebuf[i].astype(F32)
    e8[...] = tot.astype(BF)
    for r in range(1, CHIPS):
        remote(e8.at[r], rbuf.at[CHIPS - 1 - r], sem_ds.at[1], sem_dr.at[1], chip_at(r), e).start()
    backward(1, 0, None)

    got(1, "ThR", "ThL", "T1hR", "T1hL", "Gh0Y", "Gh1Y")
    forward(1, 2)
    to_mate_sum(1, 0)
    backward(1, 2, to_mate)
    give_back(0, 0)
    to_far(1, 0)
    to_far(1, 1)
    to_mate_sum(1, 1)
    to_far_again(1, 0)
    to_far_again(1, 1)

    take(rbuf, sem_dr.at[1])
    tot = e8[0].astype(F32)
    for r in range(CHIPS - 1):
        tot = tot + rbuf[r].astype(F32)
    f1[...] = tot.astype(BF)
    own_final = pltpu.make_async_copy(f1, dlat.at[rows_e, lanes_e], sem_l.at[11])
    own_final.start()
    for i in range(1, N_EXP):
        te = lax.rem(e + i, N_EXP)
        remote(f1, dlat.at[rows_e, lanes_e], sem_ds.at[9], sem_dr.at[9], c, te).start()
    dq_ref[...] = dqs[...].reshape(T_ATT, 4, LAT)

    give_back(1, 0)
    give_back(1, 1)

    own_final.wait()
    take(ebuf.at[pl.ds(0, 15), 0], sem_dr.at[9])
    dlat_ref[...] = dlat[...]

    for b in range(2):
        for arr in range(2):
            take(incoming(ra.at[arr], b), sem_as.at[2 * b + arr])
    take(kbuf.at[pl.ds(0, 7 * T_ATT), :], sem_ks.at[0])
    lat_sib.wait_send()
    for cp in rem:
        cp.wait_send()
    for cp in hops.values():
        cp.wait_send()
    for cp in swaps.values():
        cp.wait_send()
    for cp in sends.values():
        cp.wait_send()
    dk_sib.wait_send()
    take(ebuf.at[pl.ds(0, 15)], sem_ds.at[8])
    take(rbuf, sem_ds.at[1])
    take(ebuf.at[pl.ds(0, 15), 0], sem_ds.at[9])
    pltpu.make_async_copy(bsend.at[0, 0], back_ref.at[0], sem_l.at[12]).wait()
    for sems in (sem_bs, sem_br):
        take(incoming(bsend, 0), sems.at[0])
        for h in range(2):
            take(bsend.at[1, :, :, pl.ds(*COLS[1][h])], sems.at[1 + h])


def fused(ids, prio, docs, tok, grd, wg, wu, wd, lat, q, do):
    vmem = pl.BlockSpec(memory_space=pltpu.VMEM)
    hbm = pl.BlockSpec(memory_space=pl.ANY)
    dma = pltpu.SemaphoreType.DMA

    def v(*shape, dtype=BF):
        return pltpu.VMEM(shape, dtype)

    return pl.pallas_call(
        kernel,
        out_shape=(
            jax.ShapeDtypeStruct((PAIRS, 2, OUTW), BF),
            jax.ShapeDtypeStruct((T_ATT, 4, LAT), BF),
            jax.ShapeDtypeStruct((T_ATT, LAT), BF),
        ),
        in_specs=[vmem] * 3 + [hbm] * 8,
        out_specs=(vmem, vmem, vmem),
        scratch_shapes=[
            v(2, 128, D),
            v(2, N_EXP, 2, D),
            v(2, 2, 16, 2, HALF),
            v(2, 2, N_X, 2 * HB, HALF),
            v(HALF, HID2),
            v(HALF, HID2),
            v(HID2, HALF),
            v(2, N_X, 3, 2 * HB, HID2, dtype=F32),
            v(2, N_X, 3, 2 * HB, HID2, dtype=F32),
            v(2 * HB, HID2),
            v(2 * HB, HID2),
            v(2, N_X, 2 * HB, OUTW),
            v(2, 2, 2 * HB, OUTW),
            v(2, HB, OUTW),
            v(2, HB, OUTW),
            v(2, 2, HB // 2, OUTW),
            v(2, HB, OUTW),
            v(2, HB, OUTW),
            v(2, HB, OUTW),
            v(2, 16, 2, OUTW),
            v(T_ATT, 4, LAT),
            v(T_ATT, 4, LAT),
            v(ROWS_ATT, LAT),
            v(ROWS_ATT, LAT),
            v(ROWS_ATT, 128),
            v(ROWS_ATT, LAT),
            v(16 * T_ATT, KW),
            v(ROWS_ATT, 16 * T_ATT),
            v(ROWS_ATT, 16 * T_ATT),
            v(16 * T_ATT, LAT, dtype=F32),
            v(16 * T_ATT, LAT),
            v(CHIPS * T_ATT, LAT),
            v(CHIPS, T_ATT, LAT),
            v(16, CHIPS, 16, 128),
            v(CHIPS, 16, 128),
            v(CHIPS - 1, 16, 128),
            v(16, 128),
            v(T_ATT, LAT),
            dma((13,)),
            dma((4,)),
            dma((4,)),
            dma((2,)),
            dma((2,)),
            dma((3,)),
            dma((3,)),
            dma((36,)),
            dma((36,)),
            dma((8,)),
            dma((8,)),
            dma((24,)),
            dma((24,)),
            dma((3,)),
            dma((3,)),
            dma((10,)),
            dma((10,)),
        ],
        compiler_params=pltpu.CompilerParams(
            collective_id=0, has_side_effects=True, vmem_limit_bytes=58 * 1024 * 1024
        ),
        name="fused",
    )(ids, prio, docs, tok, grd, wg, wu, wd, lat, q, do)


def combine_kernel(ids_ref, prio_ref, gv_ref, back_ref, dq_in, dlat_in, dtok_ref, dg_ref, dq_ref, dlat_ref):
    ids = ids_ref[...]
    chosen, expert = route(ids, prio_ref[...])
    weight = jnp.zeros((PAIRS, 128), F32)
    for k in range(8):
        weight = weight + jnp.where(ids[k : k + 1, :] == expert, gv_ref[k : k + 1, :], 0.0)
    weight = weight * chosen
    w1 = weight.astype(BF).astype(F32)
    w2 = (weight - w1).astype(BF).astype(F32)
    w3 = weight - w1 - w2
    terms = jnp.concatenate([w3, w2, w1, jnp.zeros((PAIRS, 128), F32)], axis=0).T.astype(BF)
    for t in range(HALF // 512):
        rows = back_ref[:, :, pl.ds(EXTRA + t * 512, 512)].reshape(PAIRS, 512)
        stacked = jnp.concatenate([rows, rows, rows, rows], axis=0)
        dtok_ref[:, pl.ds(t * 512, 512)] = nn(terms, stacked).astype(BF)

    @pl.when(pl.program_id(0) == 0)
    def _():
        score = back_ref[:, :, pl.ds(0, EXTRA)].reshape(PAIRS, EXTRA).astype(F32)
        kept = chosen * score
        for k in range(8):
            own = jnp.where(ids[k : k + 1, :] == expert, kept, 0.0)
            dg_ref[k : k + 1, :] = jnp.sum(own, axis=0, keepdims=True).astype(BF)
        dq_ref[...] = dq_in[...]
        dlat_ref[...] = dlat_in[...]


def combine(ids, prio, gv, back, dq, dlat):
    def whole(shape):
        return pl.BlockSpec(shape, lambda h: (0,) * len(shape))

    return pl.pallas_call(
        combine_kernel,
        grid=(2,),
        out_shape=(
            jax.ShapeDtypeStruct((128, D), BF),
            jax.ShapeDtypeStruct((8, 128), BF),
            jax.ShapeDtypeStruct(dq.shape, BF),
            jax.ShapeDtypeStruct(dlat.shape, BF),
        ),
        in_specs=[
            whole((8, 128)),
            whole((1, 128)),
            whole((8, 128)),
            pl.BlockSpec((N_EXP, 2, OUTW), lambda h: (h, 0, 0)),
            whole(dq.shape),
            whole(dlat.shape),
        ],
        out_specs=(
            pl.BlockSpec((128, HALF), lambda h: (0, h)),
            whole((8, 128)),
            whole(dq.shape),
            whole(dlat.shape),
        ),
        name="combine",
    )(ids, prio, gv, back, dq, dlat)


def local(
    queries,
    latent,
    grad_out,
    doc_ids,
    tokens,
    token_grads,
    gate_values,
    expert_ids,
    gate_order,
    w_gate,
    w_up,
    w_down,
):
    ids = expert_ids.T
    back, dq, dlat = fused(
        ids,
        gate_order,
        doc_ids.reshape(1, T_ATT),
        tokens,
        token_grads,
        w_gate[0],
        w_up[0],
        w_down[0],
        latent,
        queries,
        grad_out,
    )
    d_tokens, d_gates, dq, dlat = combine(ids, gate_order, gate_values.T, back, dq, dlat)
    return (dq, dlat, d_tokens, d_gates.T)


def solution(mesh):
    in_specs = (
        P("ctx", "exp", None),
        P("ctx", None),
        P("ctx", "exp", None),
        P("ctx"),
        P(("ctx", "exp"), None),
        P(("ctx", "exp"), None),
        P(("ctx", "exp"), None),
        P(("ctx", "exp"), None),
        P(("ctx", "exp"), None),
        P("exp", None, "ctx"),
        P("exp", None, "ctx"),
        P("exp", "ctx", None),
    )
    out_specs = (
        P("ctx", "exp", None),
        P("ctx", None),
        P(("ctx", "exp"), None),
        P(("ctx", "exp"), None),
    )
    return jax.shard_map(local, mesh=mesh, in_specs=in_specs, out_specs=out_specs, check_vma=False)
```

```python
import jax
import jax.numpy as jnp
from jax import lax
from jax.experimental import pallas as pl
from jax.experimental.pallas import tpu as pltpu
from jax.sharding import PartitionSpec as P

SCALE = 192 ** (-0.5)
MESH = pl.DeviceIdType.MESH
BF = jnp.bfloat16
F32 = jnp.float32

N_X, N_CORE = 4, 2
N_EXP = 16
CHIPS = 8
D = 7168
HALF = D // 2
SHARD = 128
HID2 = 2 * SHARD
LAT = 512
KW = LAT + 128
T_ATT = 64
ROWS_ATT = 256
BLK = 64
PAIRS = 32
EXTRA = 128
OUTW = EXTRA + HALF
STEP = 256
HB = BLK // 2
OFFSETS = (0, 1, -1, 2, -2, 3, -3, 4, -4, 5, -5, 6, -6, 7, -7, 8)
COLS = (((0, OUTW),), ((0, EXTRA + HALF // 2), (EXTRA + HALF // 2, HALF // 2)))


def nt(a, b):
    return lax.dot_general(a, b, (((1,), (1,)), ((), ())), preferred_element_type=F32)


def nn(a, b):
    return lax.dot_general(a, b, (((1,), (0,)), ((), ())), preferred_element_type=F32)


def tn(a, b):
    return lax.dot_general(a, b, (((0,), (0,)), ((), ())), preferred_element_type=F32)


def route(ids, prio):
    pair = lax.broadcasted_iota(jnp.int32, (PAIRS, 128), 0)
    expert = lax.shift_right_logical(pair, 1)
    slot = (pair - 2 * expert).astype(F32)
    hits = jnp.zeros((PAIRS, 128), F32)
    for k in range(8):
        hits = hits + jnp.where(ids[k : k + 1, :] == expert, 1.0, 0.0)
    later = jnp.broadcast_to(prio.astype(F32), (128, 128))
    earlier = jnp.where(later.T < later, 1.0, 0.0)
    ranks = nn(hits.astype(BF), earlier.astype(BF))
    chosen = jnp.where((hits == 1.0) & (ranks == slot), 1.0, 0.0)
    return chosen, expert


def split_score(score):
    hi = score.astype(BF).astype(F32)
    lane = lax.broadcasted_iota(jnp.int32, (score.shape[0], EXTRA), 1)
    return jnp.where(lane == 0, hi, jnp.where(lane == 1, score - hi, 0.0)).astype(BF)


def kernel(
    ids_ref, prio_ref, docs_ref, tok_hbm, grd_hbm, wg_hbm, wu_hbm, wd_hbm, lat_hbm, q_hbm, do_hbm,
    back_ref, dq_ref, dlat_ref,
    rows_v, snd, ra, xg, wg, wu, wd, pbuf, prec, ggb, ugb, parts, rsx, rsm, s2p, rsf, rs2, ysend, rsy, bsend,
    q3, do3, qs, dos, qd, dqs, kbuf, dsb, pwb, dkf, dkb, drec, s2b, ebuf, e8, rbuf, f1, gbuf,
    sem_l, sem_as, sem_ar, sem_ks, sem_kr, sem_ws, sem_wr, sem_gs, sem_gr, sem_ps, sem_pr,
    sem_rs, sem_rr, sem_bs, sem_br, sem_ds, sem_dr,
):
    c = lax.axis_index("ctx")
    e = lax.axis_index("exp")
    core = lax.rem(c, 2)
    chip = lax.div(c, 2)
    y = lax.rem(chip, 2)
    x = lax.div(chip, 2)
    sib = c + 1 - 2 * core
    other = 1 - core
    right = 4 * lax.rem(x + 1, N_X) + 2 * y + core
    left = 4 * lax.rem(x + 3, N_X) + 2 * y + core
    mate = 4 * x + 2 * (1 - y) + core

    def at(ctx, exp):
        return {"ctx": ctx, "exp": exp}

    def remote(src, dst, ssem, rsem, ctx, exp):
        return pltpu.make_async_remote_copy(
            src_ref=src,
            dst_ref=dst,
            send_sem=ssem,
            recv_sem=rsem,
            device_id=at(ctx, exp),
            device_id_type=MESH,
        )

    def take(ref, sem):
        pltpu.make_async_copy(ref, ref, sem).wait()

    def entry(off, k):
        tc = lax.rem(core + k, 2)
        base = mate - core if off % 2 else 2 * chip
        return base + tc, tc

    def chip_at(r):
        return 2 * lax.rem(chip + r, CHIPS) + core

    lane0 = pl.multiple_of(core * SHARD, SHARD)
    own_d = pl.ds(pl.multiple_of(core * HALF, HALF), HALF)
    oth_d = pl.ds(pl.multiple_of(other * HALF, HALF), HALF)
    own_k = pl.ds(pl.multiple_of(core * 512, 512), 512)
    oth_k = pl.ds(pl.multiple_of(other * 512, 512), 512)
    own_b = pl.ds(pl.multiple_of(core * 512, 512), T_ATT)
    rows_in = [
        pltpu.make_async_copy(tok_hbm, rows_v.at[0], sem_l.at[0]),
        pltpu.make_async_copy(grd_hbm, rows_v.at[1], sem_l.at[1]),
    ]
    lat_in = pltpu.make_async_copy(lat_hbm, kbuf.at[own_b, pl.ds(0, LAT)], sem_l.at[2])
    att_in = [
        pltpu.make_async_copy(q_hbm, q3, sem_l.at[3]),
        pltpu.make_async_copy(do_hbm, do3, sem_l.at[4]),
    ]
    w_in = [
        pltpu.make_async_copy(wg_hbm.at[own_d, :], wg.at[:, pl.ds(lane0, SHARD)], sem_l.at[5]),
        pltpu.make_async_copy(wu_hbm.at[own_d, :], wu.at[:, pl.ds(lane0, SHARD)], sem_l.at[6]),
        pltpu.make_async_copy(wd_hbm.at[:, own_d], wd.at[pl.ds(lane0, SHARD), :], sem_l.at[7]),
    ]
    rows_in[0].start()
    lat_in.start()
    rows_in[1].start()

    bar = pltpu.get_barrier_semaphore()
    pl.semaphore_signal(bar, inc=1, device_id=at(sib, e), device_id_type=MESH)
    for r in range(1, CHIPS):
        pl.semaphore_signal(bar, inc=1, device_id=at(chip_at(r), e), device_id_type=MESH)
    for i in range(1, N_EXP):
        te = lax.rem(e + i, N_EXP)
        for k in range(N_CORE):
            pl.semaphore_signal(bar, inc=1, device_id=at(entry(i, k)[0], te), device_id_type=MESH)
        if i % 2:
            pl.semaphore_signal(bar, inc=1, device_id=at(c, te), device_id_type=MESH)
    for cp in att_in + w_in:
        cp.start()

    chosen, _ = route(ids_ref[...], prio_ref[...])
    picker = chosen.astype(BF)

    def pick(arr):
        rows_in[arr].wait()

        def body(t, carry):
            cols = pl.ds(pl.multiple_of(t * 512, 512), 512)
            val = nn(picker, rows_v[arr, :, cols]).astype(BF)
            snd[arr, :, :, cols] = val.reshape(N_EXP, 2, 512)
            return carry

        lax.fori_loop(0, D // 512, body, 0)

    def scatter(arr, b):
        for p in range(8):
            te = lax.rem(e + (N_EXP - OFFSETS[8 * b + p]) % N_EXP, N_EXP)
            for k in range(N_CORE):
                to, tc = entry(OFFSETS[8 * b + p], k)
                src = snd.at[arr, te, :, pl.ds(pl.multiple_of(tc * HALF, HALF), HALF)]
                dst = ra.at[arr, b, core * 8 + p]
                if b == 0 and p == 0 and k == 0:
                    pltpu.make_async_copy(src, dst, sem_l.at[8 + arr]).start()
                else:
                    sem = 2 * b + arr
                    remote(src, dst, sem_as.at[sem], sem_ar.at[sem], to, te).start()

    def incoming(buf, b):
        return buf.at[b, pl.ds(0, 15 + b)]

    pick(0)
    doc = lax.broadcasted_iota(jnp.int32, (128, T_ATT), 0)
    onehot_t = jnp.where(docs_ref[...] == doc, 1.0, 0.0).astype(BF)
    eye = jnp.where(
        lax.broadcasted_iota(jnp.int32, (128, 128), 0) == lax.broadcasted_iota(jnp.int32, (128, 128), 1),
        1.0,
        0.0,
    ).astype(BF)
    onehot = tn(onehot_t, eye).astype(BF)
    kbuf[own_b, pl.ds(LAT, 128)] = onehot
    lat_in.wait()

    pl.semaphore_wait(bar, 1 + 7 + 30 + 8)

    for r in range(1, CHIPS):
        row = core * 512 + (CHIPS - r) * T_ATT
        dst = kbuf.at[pl.ds(pl.multiple_of(row, T_ATT), T_ATT), :]
        remote(kbuf.at[own_b, :], dst, sem_ks.at[0], sem_kr.at[0], chip_at(r), e).start()
    scatter(0, 0)
    pick(1)
    scatter(1, 0)
    scatter(0, 1)
    scatter(1, 1)
    rem = [
        remote(wg_hbm.at[oth_d, :], wg.at[:, pl.ds(lane0, SHARD)], sem_ws.at[0], sem_wr.at[0], sib, e),
        remote(wu_hbm.at[oth_d, :], wu.at[:, pl.ds(lane0, SHARD)], sem_ws.at[1], sem_wr.at[1], sib, e),
        remote(wd_hbm.at[:, oth_d], wd.at[pl.ds(lane0, SHARD), :], sem_ws.at[2], sem_wr.at[2], sib, e),
    ]
    for cp in rem:
        cp.start()

    for cp in att_in:
        cp.wait()
    qs[...] = q3[...].reshape(ROWS_ATT, LAT)
    dos[...] = do3[...].reshape(ROWS_ATT, LAT)
    row_q = lax.shift_right_logical(lax.broadcasted_iota(jnp.int32, (ROWS_ATT, T_ATT), 0), 2)
    col_q = lax.broadcasted_iota(jnp.int32, (ROWS_ATT, T_ATT), 1)
    qd[...] = nn(jnp.where(row_q == col_q, 1.0, 0.0).astype(BF), onehot).astype(BF)

    hops = {}
    names = {}

    def hop(b, name, arr, dx, dy, way, lo=0, n=HB):
        if way == "R":
            to, tx, ty = right, (dx + 3) % 4, dy
        elif way == "L":
            to, tx, ty = left, (dx + 1) % 4, dy
        else:
            to, tx, ty = mate, dx, 1 - dy
        index = 18 * b + names.setdefault(name, len(names))
        hops[b, name] = remote(
            xg.at[arr, b, dx, pl.ds(dy * HB + lo, n), :],
            xg.at[arr, b, tx, pl.ds(ty * HB + lo, n), :],
            sem_gs.at[index],
            sem_gr.at[index],
            to,
            e,
        )
        hops[b, name].start()

    def got(b, *which):
        for name in which:
            hops[b, name].wait_recv()

    def repack(arr, b):
        if b == 0:
            pltpu.make_async_copy(
                snd.at[0, 0, :, pl.ds(0, HALF)], ra.at[arr, 0, 0], sem_l.at[8 + arr]
            ).wait()
        take(incoming(ra.at[arr], b), sem_ar.at[2 * b + arr])

        def body(t, carry):
            cols = pl.ds(pl.multiple_of(t * 512, 512), 512)
            xg[arr, b, 0, pl.ds(0, HB), cols] = ra[arr, b, :, :, cols].reshape(HB, 512)
            return carry

        lax.fori_loop(0, HALF // 512, body, 0)

    def hops_own(b):
        repack(0, b)
        hop(b, "TY", 0, 0, 0, "Y")
        hop(b, "TR", 0, 0, 0, "R")
        hop(b, "TL", 0, 0, 0, "L")
        repack(1, b)
        hop(b, "GR", 1, 0, 0, "R")
        hop(b, "GL", 1, 0, 0, "L")
        hop(b, "GY", 1, 0, 0, "Y")

    def hops_second(b):
        got(b, "TY")
        hop(b, "T1R", 0, 0, 1, "R")
        hop(b, "T1L", 0, 0, 1, "L")
        got(b, "GR", "GL")
        hop(b, "GlY", 1, 3, 0, "Y")
        hop(b, "GrY", 1, 1, 0, "Y")
        hop(b, "GhR", 1, 3, 0, "R", 0, HB // 2)
        hop(b, "GhL", 1, 1, 0, "L", HB // 2, HB // 2)
        got(b, "TR", "TL")
        hop(b, "ThR", 0, 3, 0, "R", 0, HB // 2)
        hop(b, "ThL", 0, 1, 0, "L", HB // 2, HB // 2)

    def hops_third(b):
        got(b, "GhR", "GhL")
        hop(b, "Gh0Y", 1, 2, 0, "Y", 0, HB // 2)
        hop(b, "Gh1Y", 1, 2, 0, "Y", HB // 2, HB // 2)
        got(b, "T1R", "T1L")
        hop(b, "T1hR", 0, 3, 1, "R", 0, HB // 2)
        hop(b, "T1hL", 0, 1, 1, "L", HB // 2, HB // 2)

    hops_own(0)
    take(kbuf.at[pl.ds(0, 7 * T_ATT), :], sem_kr.at[0])
    lat_sib = remote(kbuf.at[own_k, :], kbuf.at[own_k, :], sem_ks.at[1], sem_kr.at[1], sib, e)
    lat_sib.start()

    lat_sib.wait_recv()

    def att(h, carry):
        rows = pl.ds(pl.multiple_of(h * 64, 64), 64)
        keys = kbuf[:, :LAT]
        same = nt(qd[rows, :], kbuf[:, LAT:])
        s = nt(qs[rows, :], keys) * SCALE
        s = jnp.where(same > 0.5, s, -1e30)
        m = jnp.max(s, axis=1, keepdims=True)
        p = jnp.exp(s - m)
        total = jnp.sum(p, axis=1, keepdims=True)
        dp = nt(dos[rows, :], keys)
        delta = jnp.sum(p.astype(BF).astype(F32) * dp, axis=1, keepdims=True) / total
        probs = p / total
        ds = (probs * (dp - delta)).astype(BF)
        dsb[rows, :] = ds
        pwb[rows, :] = probs.astype(BF)
        dqs[rows, :] = (nn(ds, keys) * SCALE).astype(BF)
        return carry

    lax.fori_loop(0, ROWS_ATT // 64, att, 0)

    hops_second(0)

    def dkeys(k, carry):
        rows = pl.ds(pl.multiple_of(k * 128, 128), 128)
        val = tn(dsb[:, rows], qs[...]) * SCALE + tn(pwb[:, rows], dos[...])
        dkf[rows, :] = val
        dkb[rows, :] = val.astype(BF)
        return carry

    lax.fori_loop(0, CHIPS, dkeys, 0)
    dk_sib = remote(dkb.at[oth_k, :], drec, sem_ds.at[0], sem_dr.at[0], sib, e)
    dk_sib.start()

    for cp in w_in:
        cp.wait()
    for cp in rem:
        cp.wait_recv()

    swaps = {}

    def forward(b, dx):
        xt, xd = xg[0, b, dx], xg[1, b, dx]
        pbuf[b, dx, 0] = nn(xt, wg[...])
        pbuf[b, dx, 1] = nn(xt, wu[...])
        pbuf[b, dx, 2] = nt(xd, wd[...])
        index = 4 * b + dx
        swaps[b, dx] = remote(
            pbuf.at[b, dx], prec.at[b, dx], sem_ps.at[index], sem_pr.at[index], sib, e
        )
        swaps[b, dx].start()

    sends = {}

    def pass_on(kind, b, h, src, dst, to):
        index = 3 * kind + b + h
        cols = pl.ds(*COLS[b][h])
        sends[kind, b, h] = remote(
            src.at[:, cols], dst.at[:, cols], sem_rs.at[index], sem_rr.at[index], to, e
        )
        sends[kind, b, h].start()

    def passed(kind, b, h):
        sends[kind, b, h].wait_recv()

    def wide(b, h):
        start, n = COLS[b][h]
        first = max(start - EXTRA, 0)
        return first, (start + n - EXTRA - first) // STEP

    def backward(b, dx, done):
        swaps[b, dx].wait_recv()
        gate = pbuf[b, dx, 0] + prec[b, dx, 0]
        up = pbuf[b, dx, 1] + prec[b, dx, 1]
        act = pbuf[b, dx, 2] + prec[b, dx, 2]
        sig = 1.0 / (1.0 + jnp.exp(-gate))
        silu = gate * sig
        hid = (silu * up).astype(BF).astype(F32)
        parts[b, dx, :, pl.ds(0, EXTRA)] = split_score(jnp.sum(hid * act, axis=1, keepdims=True))
        ggb[...] = (act * up * sig * (1.0 + gate * (1.0 - sig))).astype(BF)
        ugb[...] = (act * silu).astype(BF)
        for h in range(len(COLS[b])):
            first, steps = wide(b, h)

            def body(t, carry):
                at_col = first + t * STEP
                cols = pl.ds(pl.multiple_of(at_col, STEP), STEP)
                val = nt(ggb[...], wg[cols, :]) + nt(ugb[...], wu[cols, :])
                parts[b, dx, :, pl.ds(pl.multiple_of(EXTRA + at_col, 128), STEP)] = val.astype(BF)
                return carry

            lax.fori_loop(0, steps, body, 0)
            if done is not None:
                done(b, h)

    def merge(b, h, put, put_score, srcs):
        def summed(cols):
            val = srcs[0][:, cols].astype(F32)
            for ref in srcs[1:]:
                val = val + ref[:, cols].astype(F32)
            return val

        if h == 0:
            put_score(jnp.sum(summed(pl.ds(0, EXTRA)), axis=1, keepdims=True))
        first, steps = wide(b, h)

        def body(t, carry):
            cols = pl.ds(pl.multiple_of(EXTRA + first + t * STEP, 128), STEP)
            put(cols, summed(cols).astype(BF))
            return carry

        lax.fori_loop(0, steps, body, 0)

    def merge_into(b, h, dst, srcs):
        def put(cols, val):
            dst[:, cols] = val

        def put_score(score):
            dst[:, pl.ds(0, EXTRA)] = split_score(score)

        merge(b, h, put, put_score, srcs)

    mine, theirs = pl.ds(0, HB), pl.ds(HB, HB)
    lo, hi = pl.ds(0, HB // 2), pl.ds(HB // 2, HB // 2)

    def to_right(b, h):
        pass_on(0, b, h, parts.at[b, 1], rsx.at[b, 0], right)

    def to_left(b, h):
        pass_on(1, b, h, parts.at[b, 3], rsx.at[b, 1], left)

    def to_mate(b, h):
        pass_on(2, b, h, parts.at[b, 2, theirs], rsm.at[b], mate)

    def to_mate_sum(b, h):
        passed(0, b, h)
        passed(1, b, h)
        merge_into(
            b, h, ysend.at[b], [parts.at[b, 0, theirs], rsx.at[b, 0, theirs], rsx.at[b, 1, theirs]]
        )
        pass_on(3, b, h, ysend.at[b], rsy.at[b], mate)

    def to_far(b, h):
        passed(2, b, h)
        merge_into(b, h, s2p.at[b], [parts.at[b, 2, mine], rsm.at[b]])
        pass_on(4, b, h, s2p.at[b, lo], rsf.at[b, 0], right)
        pass_on(5, b, h, s2p.at[b, hi], rsf.at[b, 1], left)

    def to_far_again(b, h):
        passed(4, b, h)
        pass_on(6, b, h, rsf.at[b, 0], rs2.at[b, lo], right)
        passed(5, b, h)
        pass_on(7, b, h, rsf.at[b, 1], rs2.at[b, hi], left)

    def give_back(b, h):
        def put(cols, val):
            bsend[b, :, :, cols] = val.reshape(16, 2, STEP)

        def put_score(score):
            val = jnp.broadcast_to(score, (HB, EXTRA)).astype(BF)
            bsend[b, :, :, pl.ds(0, EXTRA)] = val.reshape(16, 2, EXTRA)

        passed(3, b, h)
        passed(6, b, h)
        passed(7, b, h)
        merge(
            b,
            h,
            put,
            put_score,
            [parts.at[b, 0, mine], rsx.at[b, 0, mine], rsx.at[b, 1, mine], rsy.at[b], rs2.at[b]],
        )
        cols = pl.ds(*COLS[b][h])
        for p in range(8):
            te = lax.rem(e + OFFSETS[8 * b + p] % N_EXP, N_EXP)
            for k in range(N_CORE):
                to, tc = entry(OFFSETS[8 * b + p], k)
                src = bsend.at[b, tc * 8 + p, :, cols]
                dst = back_ref.at[core * N_EXP + e, :, cols]
                if b == 0 and p == 0 and k == 0:
                    pltpu.make_async_copy(src, dst, sem_l.at[12]).start()
                else:
                    remote(src, dst, sem_bs.at[b + h], sem_br.at[b + h], to, te).start()

    got(0, "GY")
    forward(0, 0)
    hops_own(1)
    hops_third(0)

    dk_sib.wait_recv()
    s2b[...] = (dkf[own_k, :] + drec[...].astype(F32)).astype(BF).reshape(CHIPS, T_ATT, LAT)

    def piece(z):
        return (
            pl.ds(pl.multiple_of(lax.div(z, 2) * 16, 16), 16),
            pl.ds(pl.multiple_of(lax.rem(z, 2) * 256, 256), 256),
        )

    rows_e, lanes_e = piece(lax.div(e, 2))
    own_piece = pltpu.make_async_copy(s2b.at[:, rows_e, lanes_e], ebuf.at[7], sem_l.at[10])
    own_piece.start()
    for i in range(1, 8):
        te = lax.rem(e + 2 * i, N_EXP)
        rows_t, lanes_t = piece(lax.div(te, 2))
        remote(s2b.at[:, rows_t, lanes_t], ebuf.at[i - 1], sem_ds.at[8], sem_dr.at[8], c, te).start()

    got(0, "GlY")
    forward(0, 3)
    got(0, "GrY")
    forward(0, 1)
    backward(0, 3, to_left)
    backward(0, 1, to_right)
    hops_second(1)
    got(0, "ThR", "ThL", "T1hR", "T1hL", "Gh0Y", "Gh1Y")
    forward(0, 2)
    backward(0, 0, None)
    backward(0, 2, to_mate)
    got(1, "GY")
    forward(1, 0)
    hops_third(1)
    to_mate_sum(0, 0)
    to_far(0, 0)
    got(1, "GlY")
    forward(1, 3)
    got(1, "GrY")
    forward(1, 1)
    backward(1, 3, to_left)
    backward(1, 1, to_right)
    to_far_again(0, 0)

    own_piece.wait()
    take(ebuf.at[pl.ds(0, 7)], sem_dr.at[8])
    tot = ebuf[0].astype(F32)
    for i in range(1, 8):
        tot = tot + ebuf[i].astype(F32)
    e8[...] = tot.astype(BF)
    for r in range(1, CHIPS):
        remote(e8.at[r], rbuf.at[CHIPS - 1 - r], sem_ds.at[1], sem_dr.at[1], chip_at(r), e).start()
    backward(1, 0, None)

    got(1, "ThR", "ThL", "T1hR", "T1hL", "Gh0Y", "Gh1Y")
    forward(1, 2)
    to_mate_sum(1, 0)
    backward(1, 2, to_mate)
    give_back(0, 0)
    to_far(1, 0)
    to_far(1, 1)
    to_mate_sum(1, 1)
    to_far_again(1, 0)
    to_far_again(1, 1)

    take(rbuf, sem_dr.at[1])
    tot = e8[0].astype(F32)
    for r in range(CHIPS - 1):
        tot = tot + rbuf[r].astype(F32)
    f1[...] = tot.astype(BF)
    own_final = pltpu.make_async_copy(f1, gbuf.at[e], sem_l.at[11])
    own_final.start()
    for i in range(1, N_EXP):
        te = lax.rem(e + i, N_EXP)
        remote(f1, gbuf.at[e], sem_ds.at[9], sem_dr.at[9], c, te).start()
    dq_ref[...] = dqs[...].reshape(T_ATT, 4, LAT)

    give_back(1, 0)
    give_back(1, 1)

    own_final.wait()
    take(gbuf.at[pl.ds(0, 15)], sem_dr.at[9])
    for z in range(8):
        both = gbuf[2 * z].astype(F32) + gbuf[2 * z + 1].astype(F32)
        dlat_ref[pl.ds(z // 2 * 16, 16), pl.ds(z % 2 * 256, 256)] = both.astype(BF)

    for b in range(2):
        for arr in range(2):
            take(incoming(ra.at[arr], b), sem_as.at[2 * b + arr])
    take(kbuf.at[pl.ds(0, 7 * T_ATT), :], sem_ks.at[0])
    lat_sib.wait_send()
    for cp in rem:
        cp.wait_send()
    for cp in hops.values():
        cp.wait_send()
    for cp in swaps.values():
        cp.wait_send()
    for cp in sends.values():
        cp.wait_send()
    dk_sib.wait_send()
    take(ebuf.at[pl.ds(0, 7)], sem_ds.at[8])
    take(rbuf, sem_ds.at[1])
    take(gbuf.at[pl.ds(0, 15)], sem_ds.at[9])
    pltpu.make_async_copy(bsend.at[0, 0], back_ref.at[0], sem_l.at[12]).wait()
    for sems in (sem_bs, sem_br):
        take(incoming(bsend, 0), sems.at[0])
        for h in range(2):
            take(bsend.at[1, :, :, pl.ds(*COLS[1][h])], sems.at[1 + h])


def fused(ids, prio, docs, tok, grd, wg, wu, wd, lat, q, do):
    vmem = pl.BlockSpec(memory_space=pltpu.VMEM)
    hbm = pl.BlockSpec(memory_space=pl.ANY)
    dma = pltpu.SemaphoreType.DMA

    def v(*shape, dtype=BF):
        return pltpu.VMEM(shape, dtype)

    return pl.pallas_call(
        kernel,
        out_shape=(
            jax.ShapeDtypeStruct((PAIRS, 2, OUTW), BF),
            jax.ShapeDtypeStruct((T_ATT, 4, LAT), BF),
            jax.ShapeDtypeStruct((T_ATT, LAT), BF),
        ),
        in_specs=[vmem] * 3 + [hbm] * 8,
        out_specs=(vmem, vmem, vmem),
        scratch_shapes=[
            v(2, 128, D),
            v(2, N_EXP, 2, D),
            v(2, 2, 16, 2, HALF),
            v(2, 2, N_X, 2 * HB, HALF),
            v(HALF, HID2),
            v(HALF, HID2),
            v(HID2, HALF),
            v(2, N_X, 3, 2 * HB, HID2, dtype=F32),
            v(2, N_X, 3, 2 * HB, HID2, dtype=F32),
            v(2 * HB, HID2),
            v(2 * HB, HID2),
            v(2, N_X, 2 * HB, OUTW),
            v(2, 2, 2 * HB, OUTW),
            v(2, HB, OUTW),
            v(2, HB, OUTW),
            v(2, 2, HB // 2, OUTW),
            v(2, HB, OUTW),
            v(2, HB, OUTW),
            v(2, HB, OUTW),
            v(2, 16, 2, OUTW),
            v(T_ATT, 4, LAT),
            v(T_ATT, 4, LAT),
            v(ROWS_ATT, LAT),
            v(ROWS_ATT, LAT),
            v(ROWS_ATT, 128),
            v(ROWS_ATT, LAT),
            v(16 * T_ATT, KW),
            v(ROWS_ATT, 16 * T_ATT),
            v(ROWS_ATT, 16 * T_ATT),
            v(16 * T_ATT, LAT, dtype=F32),
            v(16 * T_ATT, LAT),
            v(CHIPS * T_ATT, LAT),
            v(CHIPS, T_ATT, LAT),
            v(8, CHIPS, 16, 256),
            v(CHIPS, 16, 256),
            v(CHIPS - 1, 16, 256),
            v(16, 256),
            v(N_EXP, 16, 256),
            dma((13,)),
            dma((4,)),
            dma((4,)),
            dma((2,)),
            dma((2,)),
            dma((3,)),
            dma((3,)),
            dma((36,)),
            dma((36,)),
            dma((8,)),
            dma((8,)),
            dma((24,)),
            dma((24,)),
            dma((3,)),
            dma((3,)),
            dma((10,)),
            dma((10,)),
        ],
        compiler_params=pltpu.CompilerParams(
            collective_id=0, has_side_effects=True, vmem_limit_bytes=58 * 1024 * 1024
        ),
        name="fused",
    )(ids, prio, docs, tok, grd, wg, wu, wd, lat, q, do)


def combine_kernel(ids_ref, prio_ref, gv_ref, back_ref, dq_in, dlat_in, dtok_ref, dg_ref, dq_ref, dlat_ref):
    ids = ids_ref[...]
    chosen, expert = route(ids, prio_ref[...])
    weight = jnp.zeros((PAIRS, 128), F32)
    for k in range(8):
        weight = weight + jnp.where(ids[k : k + 1, :] == expert, gv_ref[k : k + 1, :], 0.0)
    weight = weight * chosen
    w1 = weight.astype(BF).astype(F32)
    w2 = (weight - w1).astype(BF).astype(F32)
    w3 = weight - w1 - w2
    terms = jnp.concatenate([w3, w2, w1, jnp.zeros((PAIRS, 128), F32)], axis=0).T.astype(BF)
    for t in range(HALF // 512):
        rows = back_ref[:, :, pl.ds(EXTRA + t * 512, 512)].reshape(PAIRS, 512)
        stacked = jnp.concatenate([rows, rows, rows, rows], axis=0)
        dtok_ref[:, pl.ds(t * 512, 512)] = nn(terms, stacked).astype(BF)

    @pl.when(pl.program_id(0) == 0)
    def _():
        score = back_ref[:, :, pl.ds(0, EXTRA)].reshape(PAIRS, EXTRA).astype(F32)
        kept = chosen * score
        for k in range(8):
            own = jnp.where(ids[k : k + 1, :] == expert, kept, 0.0)
            dg_ref[k : k + 1, :] = jnp.sum(own, axis=0, keepdims=True).astype(BF)
        dq_ref[...] = dq_in[...]
        dlat_ref[...] = dlat_in[...]


def combine(ids, prio, gv, back, dq, dlat):
    def whole(shape):
        return pl.BlockSpec(shape, lambda h: (0,) * len(shape))

    return pl.pallas_call(
        combine_kernel,
        grid=(2,),
        out_shape=(
            jax.ShapeDtypeStruct((128, D), BF),
            jax.ShapeDtypeStruct((8, 128), BF),
            jax.ShapeDtypeStruct(dq.shape, BF),
            jax.ShapeDtypeStruct(dlat.shape, BF),
        ),
        in_specs=[
            whole((8, 128)),
            whole((1, 128)),
            whole((8, 128)),
            pl.BlockSpec((N_EXP, 2, OUTW), lambda h: (h, 0, 0)),
            whole(dq.shape),
            whole(dlat.shape),
        ],
        out_specs=(
            pl.BlockSpec((128, HALF), lambda h: (0, h)),
            whole((8, 128)),
            whole(dq.shape),
            whole(dlat.shape),
        ),
        name="combine",
    )(ids, prio, gv, back, dq, dlat)


def local(
    queries,
    latent,
    grad_out,
    doc_ids,
    tokens,
    token_grads,
    gate_values,
    expert_ids,
    gate_order,
    w_gate,
    w_up,
    w_down,
):
    ids = expert_ids.T
    back, dq, dlat = fused(
        ids,
        gate_order,
        doc_ids.reshape(1, T_ATT),
        tokens,
        token_grads,
        w_gate[0],
        w_up[0],
        w_down[0],
        latent,
        queries,
        grad_out,
    )
    d_tokens, d_gates, dq, dlat = combine(ids, gate_order, gate_values.T, back, dq, dlat)
    return (dq, dlat, d_tokens, d_gates.T)


def solution(mesh):
    in_specs = (
        P("ctx", "exp", None),
        P("ctx", None),
        P("ctx", "exp", None),
        P("ctx"),
        P(("ctx", "exp"), None),
        P(("ctx", "exp"), None),
        P(("ctx", "exp"), None),
        P(("ctx", "exp"), None),
        P(("ctx", "exp"), None),
        P("exp", None, "ctx"),
        P("exp", None, "ctx"),
        P("exp", "ctx", None),
    )
    out_specs = (
        P("ctx", "exp", None),
        P("ctx", None),
        P(("ctx", "exp"), None),
        P(("ctx", "exp"), None),
    )
    return jax.shard_map(local, mesh=mesh, in_specs=in_specs, out_specs=out_specs, check_vma=False)
```

```python
import jax
import jax.numpy as jnp
from jax import lax
from jax.experimental import pallas as pl
from jax.experimental.pallas import tpu as pltpu
from jax.sharding import PartitionSpec as P

SCALE = 192 ** (-0.5)
MESH = pl.DeviceIdType.MESH
BF = jnp.bfloat16
F32 = jnp.float32

N_X, N_CORE = 4, 2
N_EXP = 16
CHIPS = 8
D = 7168
HALF = D // 2
SHARD = 128
HID2 = 2 * SHARD
LAT = 512
KW = LAT + 128
T_ATT = 64
ROWS_ATT = 256
BLK = 64
PAIRS = 32
EXTRA = 128
OUTW = EXTRA + HALF
STEP = 256
HB = BLK // 2
OFFSETS = (0, 1, -1, 2, -2, 3, -3, 4, -4, 5, -5, 6, -6, 7, -7, 8)
COLS = (((0, OUTW),), ((0, 1152), (1152, 1024), (2176, 768), (2944, 768)))
PIECES = len(COLS[0]) + len(COLS[1])


def nt(a, b):
    return lax.dot_general(a, b, (((1,), (1,)), ((), ())), preferred_element_type=F32)


def nn(a, b):
    return lax.dot_general(a, b, (((1,), (0,)), ((), ())), preferred_element_type=F32)


def tn(a, b):
    return lax.dot_general(a, b, (((0,), (0,)), ((), ())), preferred_element_type=F32)


def route(ids, prio):
    pair = lax.broadcasted_iota(jnp.int32, (PAIRS, 128), 0)
    expert = lax.shift_right_logical(pair, 1)
    slot = (pair - 2 * expert).astype(F32)
    hits = jnp.zeros((PAIRS, 128), F32)
    for k in range(8):
        hits = hits + jnp.where(ids[k : k + 1, :] == expert, 1.0, 0.0)
    later = jnp.broadcast_to(prio.astype(F32), (128, 128))
    earlier = jnp.where(later.T < later, 1.0, 0.0)
    ranks = nn(hits.astype(BF), earlier.astype(BF))
    chosen = jnp.where((hits == 1.0) & (ranks == slot), 1.0, 0.0)
    return chosen, expert


def split_score(score):
    hi = score.astype(BF).astype(F32)
    lane = lax.broadcasted_iota(jnp.int32, (score.shape[0], EXTRA), 1)
    return jnp.where(lane == 0, hi, jnp.where(lane == 1, score - hi, 0.0)).astype(BF)


def kernel(
    ids_ref, prio_ref, docs_ref, tok_hbm, grd_hbm, wg_hbm, wu_hbm, wd_hbm, lat_hbm, q_hbm, do_hbm,
    back_ref, dq_ref, dlat_ref,
    rows_v, snd, ra, xg, wg, wu, wd, pbuf, prec, ggb, ugb, parts, rsx, rsd, rsm, s2p, s3p, rsf, rs2, ysend, rsy, bsend,
    q3, do3, qs, dos, qd, dqs, kbuf, dsb, pwb, dkf, dkb, drec, s2b, ebuf, e8, rbuf, f1, gbuf,
    sem_l, sem_as, sem_ar, sem_ks, sem_kr, sem_ws, sem_wr, sem_gs, sem_gr, sem_ps, sem_pr,
    sem_rs, sem_rr, sem_bs, sem_br, sem_ds, sem_dr,
):
    c = lax.axis_index("ctx")
    e = lax.axis_index("exp")
    core = lax.rem(c, 2)
    chip = lax.div(c, 2)
    y = lax.rem(chip, 2)
    x = lax.div(chip, 2)
    sib = c + 1 - 2 * core
    other = 1 - core
    right = 4 * lax.rem(x + 1, N_X) + 2 * y + core
    left = 4 * lax.rem(x + 3, N_X) + 2 * y + core
    mate = 4 * x + 2 * (1 - y) + core

    def at(ctx, exp):
        return {"ctx": ctx, "exp": exp}

    def remote(src, dst, ssem, rsem, ctx, exp):
        return pltpu.make_async_remote_copy(
            src_ref=src,
            dst_ref=dst,
            send_sem=ssem,
            recv_sem=rsem,
            device_id=at(ctx, exp),
            device_id_type=MESH,
        )

    def take(ref, sem):
        pltpu.make_async_copy(ref, ref, sem).wait()

    def entry(off, k):
        tc = lax.rem(core + k, 2)
        base = mate - core if off % 2 else 2 * chip
        return base + tc, tc

    def chip_at(r):
        return 2 * lax.rem(chip + r, CHIPS) + core

    lane0 = pl.multiple_of(core * SHARD, SHARD)
    own_d = pl.ds(pl.multiple_of(core * HALF, HALF), HALF)
    oth_d = pl.ds(pl.multiple_of(other * HALF, HALF), HALF)
    own_k = pl.ds(pl.multiple_of(core * 512, 512), 512)
    oth_k = pl.ds(pl.multiple_of(other * 512, 512), 512)
    own_b = pl.ds(pl.multiple_of(core * 512, 512), T_ATT)
    rows_in = [
        pltpu.make_async_copy(tok_hbm, rows_v.at[0], sem_l.at[0]),
        pltpu.make_async_copy(grd_hbm, rows_v.at[1], sem_l.at[1]),
    ]
    lat_in = pltpu.make_async_copy(lat_hbm, kbuf.at[own_b, pl.ds(0, LAT)], sem_l.at[2])
    att_in = [
        pltpu.make_async_copy(q_hbm, q3, sem_l.at[3]),
        pltpu.make_async_copy(do_hbm, do3, sem_l.at[4]),
    ]
    w_in = [
        pltpu.make_async_copy(wg_hbm.at[own_d, :], wg.at[:, pl.ds(lane0, SHARD)], sem_l.at[5]),
        pltpu.make_async_copy(wu_hbm.at[own_d, :], wu.at[:, pl.ds(lane0, SHARD)], sem_l.at[6]),
        pltpu.make_async_copy(wd_hbm.at[:, own_d], wd.at[pl.ds(lane0, SHARD), :], sem_l.at[7]),
    ]
    rows_in[0].start()
    lat_in.start()
    rows_in[1].start()

    bar = pltpu.get_barrier_semaphore()
    pl.semaphore_signal(bar, inc=1, device_id=at(sib, e), device_id_type=MESH)
    for r in range(1, CHIPS):
        pl.semaphore_signal(bar, inc=1, device_id=at(chip_at(r), e), device_id_type=MESH)
    for i in range(1, N_EXP):
        te = lax.rem(e + i, N_EXP)
        for k in range(N_CORE):
            pl.semaphore_signal(bar, inc=1, device_id=at(entry(i, k)[0], te), device_id_type=MESH)
        if i % 2:
            pl.semaphore_signal(bar, inc=1, device_id=at(c, te), device_id_type=MESH)
    for cp in att_in + w_in:
        cp.start()

    chosen, _ = route(ids_ref[...], prio_ref[...])
    picker = chosen.astype(BF)

    def pick(arr):
        rows_in[arr].wait()

        def body(t, carry):
            cols = pl.ds(pl.multiple_of(t * 512, 512), 512)
            val = nn(picker, rows_v[arr, :, cols]).astype(BF)
            snd[arr, :, :, cols] = val.reshape(N_EXP, 2, 512)
            return carry

        lax.fori_loop(0, D // 512, body, 0)

    def scatter(arr, b):
        for p in range(8):
            te = lax.rem(e + (N_EXP - OFFSETS[8 * b + p]) % N_EXP, N_EXP)
            for k in range(N_CORE):
                to, tc = entry(OFFSETS[8 * b + p], k)
                src = snd.at[arr, te, :, pl.ds(pl.multiple_of(tc * HALF, HALF), HALF)]
                dst = ra.at[arr, b, core * 8 + p]
                if b == 0 and p == 0 and k == 0:
                    pltpu.make_async_copy(src, dst, sem_l.at[8 + arr]).start()
                else:
                    sem = 2 * b + arr
                    remote(src, dst, sem_as.at[sem], sem_ar.at[sem], to, te).start()

    def incoming(buf, b):
        return buf.at[b, pl.ds(0, 15 + b)]

    pick(0)
    doc = lax.broadcasted_iota(jnp.int32, (128, T_ATT), 0)
    onehot_t = jnp.where(docs_ref[...] == doc, 1.0, 0.0).astype(BF)
    eye = jnp.where(
        lax.broadcasted_iota(jnp.int32, (128, 128), 0) == lax.broadcasted_iota(jnp.int32, (128, 128), 1),
        1.0,
        0.0,
    ).astype(BF)
    onehot = tn(onehot_t, eye).astype(BF)
    kbuf[own_b, pl.ds(LAT, 128)] = onehot
    lat_in.wait()

    pl.semaphore_wait(bar, 1 + 7 + 30 + 8)

    for r in range(1, CHIPS):
        row = core * 512 + (CHIPS - r) * T_ATT
        dst = kbuf.at[pl.ds(pl.multiple_of(row, T_ATT), T_ATT), :]
        remote(kbuf.at[own_b, :], dst, sem_ks.at[0], sem_kr.at[0], chip_at(r), e).start()
    scatter(0, 0)
    pick(1)
    scatter(1, 0)
    scatter(0, 1)
    scatter(1, 1)
    rem = [
        remote(wg_hbm.at[oth_d, :], wg.at[:, pl.ds(lane0, SHARD)], sem_ws.at[0], sem_wr.at[0], sib, e),
        remote(wu_hbm.at[oth_d, :], wu.at[:, pl.ds(lane0, SHARD)], sem_ws.at[1], sem_wr.at[1], sib, e),
        remote(wd_hbm.at[:, oth_d], wd.at[pl.ds(lane0, SHARD), :], sem_ws.at[2], sem_wr.at[2], sib, e),
    ]
    for cp in rem:
        cp.start()

    for cp in att_in:
        cp.wait()
    qs[...] = q3[...].reshape(ROWS_ATT, LAT)
    dos[...] = do3[...].reshape(ROWS_ATT, LAT)
    row_q = lax.shift_right_logical(lax.broadcasted_iota(jnp.int32, (ROWS_ATT, T_ATT), 0), 2)
    col_q = lax.broadcasted_iota(jnp.int32, (ROWS_ATT, T_ATT), 1)
    qd[...] = nn(jnp.where(row_q == col_q, 1.0, 0.0).astype(BF), onehot).astype(BF)

    hops = {}
    names = {}

    def hop(b, name, arr, dx, dy, way, lo=0, n=HB):
        if way == "R":
            to, tx, ty = right, (dx + 3) % 4, dy
        elif way == "L":
            to, tx, ty = left, (dx + 1) % 4, dy
        else:
            to, tx, ty = mate, dx, 1 - dy
        index = 18 * b + names.setdefault(name, len(names))
        hops[b, name] = remote(
            xg.at[arr, b, dx, pl.ds(dy * HB + lo, n), :],
            xg.at[arr, b, tx, pl.ds(ty * HB + lo, n), :],
            sem_gs.at[index],
            sem_gr.at[index],
            to,
            e,
        )
        hops[b, name].start()

    def got(b, *which):
        for name in which:
            hops[b, name].wait_recv()

    def repack(arr, b):
        if b == 0:
            pltpu.make_async_copy(
                snd.at[0, 0, :, pl.ds(0, HALF)], ra.at[arr, 0, 0], sem_l.at[8 + arr]
            ).wait()
        take(incoming(ra.at[arr], b), sem_ar.at[2 * b + arr])

        def body(t, carry):
            cols = pl.ds(pl.multiple_of(t * 512, 512), 512)
            xg[arr, b, 0, pl.ds(0, HB), cols] = ra[arr, b, :, :, cols].reshape(HB, 512)
            return carry

        lax.fori_loop(0, HALF // 512, body, 0)

    def hops_own(b):
        repack(0, b)
        hop(b, "TY", 0, 0, 0, "Y")
        hop(b, "TR", 0, 0, 0, "R")
        hop(b, "TL", 0, 0, 0, "L")
        repack(1, b)
        hop(b, "GR", 1, 0, 0, "R")
        hop(b, "GL", 1, 0, 0, "L")
        hop(b, "GY", 1, 0, 0, "Y")

    def hops_second(b):
        got(b, "TY")
        hop(b, "T1R", 0, 0, 1, "R")
        hop(b, "T1L", 0, 0, 1, "L")
        got(b, "GR", "GL")
        hop(b, "GlY", 1, 3, 0, "Y")
        hop(b, "GrY", 1, 1, 0, "Y")
        hop(b, "GhR", 1, 3, 0, "R", 0, HB // 2)
        hop(b, "GhL", 1, 1, 0, "L", HB // 2, HB // 2)
        got(b, "TR", "TL")
        hop(b, "ThR", 0, 3, 0, "R", 0, HB // 2)
        hop(b, "ThL", 0, 1, 0, "L", HB // 2, HB // 2)

    def hops_third(b):
        got(b, "GhR", "GhL")
        hop(b, "Gh0Y", 1, 2, 0, "Y", 0, HB // 2)
        hop(b, "Gh1Y", 1, 2, 0, "Y", HB // 2, HB // 2)
        got(b, "T1R", "T1L")
        hop(b, "T1hR", 0, 3, 1, "R", 0, HB // 2)
        hop(b, "T1hL", 0, 1, 1, "L", HB // 2, HB // 2)

    hops_own(0)
    take(kbuf.at[pl.ds(0, 7 * T_ATT), :], sem_kr.at[0])
    lat_sib = remote(kbuf.at[own_k, :], kbuf.at[own_k, :], sem_ks.at[1], sem_kr.at[1], sib, e)
    lat_sib.start()

    lat_sib.wait_recv()

    def att(h, carry):
        rows = pl.ds(pl.multiple_of(h * 64, 64), 64)
        keys = kbuf[:, :LAT]
        same = nt(qd[rows, :], kbuf[:, LAT:])
        s = nt(qs[rows, :], keys) * SCALE
        s = jnp.where(same > 0.5, s, -1e30)
        m = jnp.max(s, axis=1, keepdims=True)
        p = jnp.exp(s - m)
        total = jnp.sum(p, axis=1, keepdims=True)
        dp = nt(dos[rows, :], keys)
        delta = jnp.sum(p.astype(BF).astype(F32) * dp, axis=1, keepdims=True) / total
        probs = p / total
        ds = (probs * (dp - delta)).astype(BF)
        dsb[rows, :] = ds
        pwb[rows, :] = probs.astype(BF)
        dqs[rows, :] = (nn(ds, keys) * SCALE).astype(BF)
        return carry

    lax.fori_loop(0, ROWS_ATT // 64, att, 0)

    hops_second(0)

    def dkeys(k, carry):
        rows = pl.ds(pl.multiple_of(k * 128, 128), 128)
        val = tn(dsb[:, rows], qs[...]) * SCALE + tn(pwb[:, rows], dos[...])
        dkf[rows, :] = val
        dkb[rows, :] = val.astype(BF)
        return carry

    lax.fori_loop(0, CHIPS, dkeys, 0)
    dk_sib = remote(dkb.at[oth_k, :], drec, sem_ds.at[0], sem_dr.at[0], sib, e)
    dk_sib.start()

    for cp in w_in:
        cp.wait()
    for cp in rem:
        cp.wait_recv()

    swaps = {}

    def forward(b, dx):
        xt, xd = xg[0, b, dx], xg[1, b, dx]
        pbuf[b, dx, 0] = nn(xt, wg[...])
        pbuf[b, dx, 1] = nn(xt, wu[...])
        pbuf[b, dx, 2] = nt(xd, wd[...])
        index = 4 * b + dx
        swaps[b, dx] = remote(
            pbuf.at[b, dx], prec.at[b, dx], sem_ps.at[index], sem_pr.at[index], sib, e
        )
        swaps[b, dx].start()

    sends = {}

    def pass_on(kind, b, h, src, dst, to):
        index = PIECES * kind + len(COLS[0]) * b + h
        cols = pl.ds(*COLS[b][h])
        sends[kind, b, h] = remote(
            src.at[:, cols], dst.at[:, cols], sem_rs.at[index], sem_rr.at[index], to, e
        )
        sends[kind, b, h].start()

    def passed(kind, b, h):
        sends[kind, b, h].wait_recv()

    def wide(b, h):
        start, n = COLS[b][h]
        first = max(start - EXTRA, 0)
        return first, (start + n - EXTRA - first) // STEP

    def backward(b, dx, done):
        swaps[b, dx].wait_recv()
        gate = pbuf[b, dx, 0] + prec[b, dx, 0]
        up = pbuf[b, dx, 1] + prec[b, dx, 1]
        act = pbuf[b, dx, 2] + prec[b, dx, 2]
        sig = 1.0 / (1.0 + jnp.exp(-gate))
        silu = gate * sig
        hid = (silu * up).astype(BF).astype(F32)
        parts[b, dx, :, pl.ds(0, EXTRA)] = split_score(jnp.sum(hid * act, axis=1, keepdims=True))
        ggb[...] = (act * up * sig * (1.0 + gate * (1.0 - sig))).astype(BF)
        ugb[...] = (act * silu).astype(BF)
        for h in range(len(COLS[b])):
            first, steps = wide(b, h)

            def body(t, carry):
                at_col = first + t * STEP
                cols = pl.ds(pl.multiple_of(at_col, STEP), STEP)
                val = nt(ggb[...], wg[cols, :]) + nt(ugb[...], wu[cols, :])
                parts[b, dx, :, pl.ds(pl.multiple_of(EXTRA + at_col, 128), STEP)] = val.astype(BF)
                return carry

            lax.fori_loop(0, steps, body, 0)
            if done is not None:
                done(b, h)

    def merge(b, h, put, put_score, srcs):
        def summed(cols):
            val = srcs[0][:, cols].astype(F32)
            for ref in srcs[1:]:
                val = val + ref[:, cols].astype(F32)
            return val

        if h == 0:
            put_score(jnp.sum(summed(pl.ds(0, EXTRA)), axis=1, keepdims=True))
        first, steps = wide(b, h)

        def body(t, carry):
            cols = pl.ds(pl.multiple_of(EXTRA + first + t * STEP, 128), STEP)
            put(cols, summed(cols).astype(BF))
            return carry

        lax.fori_loop(0, steps, body, 0)

    def merge_into(b, h, dst, srcs):
        def put(cols, val):
            dst[:, cols] = val

        def put_score(score):
            dst[:, pl.ds(0, EXTRA)] = split_score(score)

        merge(b, h, put, put_score, srcs)

    mine, theirs = pl.ds(0, HB), pl.ds(HB, HB)
    lo, hi = pl.ds(0, HB // 2), pl.ds(HB // 2, HB // 2)

    def to_right(b, h):
        pass_on(0, b, h, parts.at[b, 1, theirs], rsx.at[b, 0], right)
        pass_on(8, b, h, parts.at[b, 1, hi], rsd.at[b, hi], right)

    def to_left(b, h):
        pass_on(1, b, h, parts.at[b, 3, theirs], rsx.at[b, 1], left)
        pass_on(9, b, h, parts.at[b, 3, lo], rsd.at[b, lo], left)

    def to_mate(b, h):
        pass_on(2, b, h, parts.at[b, 2, theirs], rsm.at[b], mate)

    def to_mate_sum(b, h):
        passed(0, b, h)
        passed(1, b, h)
        merge_into(b, h, ysend.at[b], [parts.at[b, 0, theirs], rsx.at[b, 0], rsx.at[b, 1]])
        pass_on(3, b, h, ysend.at[b], rsy.at[b], mate)

    def to_far(b, h):
        passed(2, b, h)
        merge_into(b, h, s2p.at[b], [parts.at[b, 2, mine], rsm.at[b]])
        pass_on(4, b, h, s2p.at[b, lo], rsf.at[b, 0], right)
        pass_on(5, b, h, s2p.at[b, hi], rsf.at[b, 1], left)

    def to_far_again(b, h):
        passed(4, b, h)
        merge_into(b, h, s3p.at[b, lo], [parts.at[b, 1, lo], rsf.at[b, 0]])
        pass_on(6, b, h, s3p.at[b, lo], rs2.at[b, lo], right)
        passed(5, b, h)
        merge_into(b, h, s3p.at[b, hi], [parts.at[b, 3, hi], rsf.at[b, 1]])
        pass_on(7, b, h, s3p.at[b, hi], rs2.at[b, hi], left)

    def give_back(b, h):
        def put(cols, val):
            bsend[b, :, :, cols] = val.reshape(16, 2, STEP)

        def put_score(score):
            val = jnp.broadcast_to(score, (HB, EXTRA)).astype(BF)
            bsend[b, :, :, pl.ds(0, EXTRA)] = val.reshape(16, 2, EXTRA)

        passed(8, b, h)
        passed(9, b, h)
        passed(3, b, h)
        passed(6, b, h)
        passed(7, b, h)
        merge(
            b,
            h,
            put,
            put_score,
            [parts.at[b, 0, mine], rsd.at[b], rsy.at[b], rs2.at[b]],
        )
        cols = pl.ds(*COLS[b][h])
        for p in range(8):
            te = lax.rem(e + OFFSETS[8 * b + p] % N_EXP, N_EXP)
            for k in range(N_CORE):
                to, tc = entry(OFFSETS[8 * b + p], k)
                src = bsend.at[b, tc * 8 + p, :, cols]
                dst = back_ref.at[core * N_EXP + e, :, cols]
                if b == 0 and p == 0 and k == 0:
                    pltpu.make_async_copy(src, dst, sem_l.at[12 + h]).start()
                else:
                    sem = len(COLS[0]) * b + h
                    remote(src, dst, sem_bs.at[sem], sem_br.at[sem], to, te).start()

    got(0, "GY")
    forward(0, 0)
    hops_own(1)
    hops_third(0)

    dk_sib.wait_recv()
    s2b[...] = (dkf[own_k, :] + drec[...].astype(F32)).astype(BF).reshape(CHIPS, T_ATT, LAT)

    def piece(z):
        return (
            pl.ds(pl.multiple_of(lax.div(z, 2) * 16, 16), 16),
            pl.ds(pl.multiple_of(lax.rem(z, 2) * 256, 256), 256),
        )

    rows_e, lanes_e = piece(lax.div(e, 2))
    own_piece = pltpu.make_async_copy(s2b.at[:, rows_e, lanes_e], ebuf.at[7], sem_l.at[10])
    own_piece.start()
    for i in range(1, 8):
        te = lax.rem(e + 2 * i, N_EXP)
        rows_t, lanes_t = piece(lax.div(te, 2))
        remote(s2b.at[:, rows_t, lanes_t], ebuf.at[i - 1], sem_ds.at[8], sem_dr.at[8], c, te).start()

    got(0, "GlY")
    forward(0, 3)
    got(0, "GrY")
    forward(0, 1)
    backward(0, 3, to_left)
    backward(0, 1, to_right)
    hops_second(1)
    got(0, "ThR", "ThL", "T1hR", "T1hL", "Gh0Y", "Gh1Y")
    forward(0, 2)
    backward(0, 0, None)
    backward(0, 2, to_mate)
    got(1, "GY")
    forward(1, 0)
    hops_third(1)
    for h in range(len(COLS[0])):
        to_mate_sum(0, h)
    for h in range(len(COLS[0])):
        to_far(0, h)
    got(1, "GlY")
    forward(1, 3)
    got(1, "GrY")
    forward(1, 1)
    backward(1, 3, to_left)
    backward(1, 1, to_right)
    for h in range(len(COLS[0])):
        to_far_again(0, h)

    own_piece.wait()
    take(ebuf.at[pl.ds(0, 7)], sem_dr.at[8])
    tot = ebuf[0].astype(F32)
    for i in range(1, 8):
        tot = tot + ebuf[i].astype(F32)
    e8[...] = tot.astype(BF)
    for r in range(1, CHIPS):
        remote(e8.at[r], rbuf.at[CHIPS - 1 - r], sem_ds.at[1], sem_dr.at[1], chip_at(r), e).start()
    got(1, "ThR", "ThL", "T1hR", "T1hL", "Gh0Y", "Gh1Y")
    forward(1, 2)
    backward(1, 2, to_mate)
    backward(1, 0, None)
    for h in range(len(COLS[0])):
        give_back(0, h)
    for h in range(len(COLS[1])):
        to_far(1, h)
    for h in range(len(COLS[1])):
        to_mate_sum(1, h)
    for h in range(len(COLS[1])):
        to_far_again(1, h)

    take(rbuf, sem_dr.at[1])
    tot = e8[0].astype(F32)
    for r in range(CHIPS - 1):
        tot = tot + rbuf[r].astype(F32)
    f1[...] = tot.astype(BF)
    own_final = pltpu.make_async_copy(f1, gbuf.at[e], sem_l.at[11])
    own_final.start()
    for i in range(1, N_EXP):
        te = lax.rem(e + i, N_EXP)
        remote(f1, gbuf.at[e], sem_ds.at[9], sem_dr.at[9], c, te).start()
    dq_ref[...] = dqs[...].reshape(T_ATT, 4, LAT)

    for h in range(len(COLS[1])):
        give_back(1, h)

    own_final.wait()
    take(gbuf.at[pl.ds(0, 15)], sem_dr.at[9])
    for z in range(8):
        both = gbuf[2 * z].astype(F32) + gbuf[2 * z + 1].astype(F32)
        dlat_ref[pl.ds(z // 2 * 16, 16), pl.ds(z % 2 * 256, 256)] = both.astype(BF)

    for b in range(2):
        for arr in range(2):
            take(incoming(ra.at[arr], b), sem_as.at[2 * b + arr])
    take(kbuf.at[pl.ds(0, 7 * T_ATT), :], sem_ks.at[0])
    lat_sib.wait_send()
    for cp in rem:
        cp.wait_send()
    for cp in hops.values():
        cp.wait_send()
    for cp in swaps.values():
        cp.wait_send()
    for cp in sends.values():
        cp.wait_send()
    dk_sib.wait_send()
    take(ebuf.at[pl.ds(0, 7)], sem_ds.at[8])
    take(rbuf, sem_ds.at[1])
    take(gbuf.at[pl.ds(0, 15)], sem_ds.at[9])
    for b in range(2):
        for h, (start, n) in enumerate(COLS[b]):
            cols = pl.ds(start, n)
            if b == 0:
                own = bsend.at[0, 0, :, cols], back_ref.at[0, :, cols]
                pltpu.make_async_copy(*own, sem_l.at[12 + h]).wait()
            for sems in (sem_bs, sem_br):
                take(bsend.at[b, pl.ds(0, 15 + b), :, cols], sems.at[len(COLS[0]) * b + h])


def fused(ids, prio, docs, tok, grd, wg, wu, wd, lat, q, do):
    vmem = pl.BlockSpec(memory_space=pltpu.VMEM)
    hbm = pl.BlockSpec(memory_space=pl.ANY)
    dma = pltpu.SemaphoreType.DMA

    def v(*shape, dtype=BF):
        return pltpu.VMEM(shape, dtype)

    return pl.pallas_call(
        kernel,
        out_shape=(
            jax.ShapeDtypeStruct((PAIRS, 2, OUTW), BF),
            jax.ShapeDtypeStruct((T_ATT, 4, LAT), BF),
            jax.ShapeDtypeStruct((T_ATT, LAT), BF),
        ),
        in_specs=[vmem] * 3 + [hbm] * 8,
        out_specs=(vmem, vmem, vmem),
        scratch_shapes=[
            v(2, 128, D),
            v(2, N_EXP, 2, D),
            v(2, 2, 16, 2, HALF),
            v(2, 2, N_X, 2 * HB, HALF),
            v(HALF, HID2),
            v(HALF, HID2),
            v(HID2, HALF),
            v(2, N_X, 3, 2 * HB, HID2, dtype=F32),
            v(2, N_X, 3, 2 * HB, HID2, dtype=F32),
            v(2 * HB, HID2),
            v(2 * HB, HID2),
            v(2, N_X, 2 * HB, OUTW),
            v(2, 2, HB, OUTW),
            v(2, HB, OUTW),
            v(2, HB, OUTW),
            v(2, HB, OUTW),
            v(2, HB, OUTW),
            v(2, 2, HB // 2, OUTW),
            v(2, HB, OUTW),
            v(2, HB, OUTW),
            v(2, HB, OUTW),
            v(2, 16, 2, OUTW),
            v(T_ATT, 4, LAT),
            v(T_ATT, 4, LAT),
            v(ROWS_ATT, LAT),
            v(ROWS_ATT, LAT),
            v(ROWS_ATT, 128),
            v(ROWS_ATT, LAT),
            v(16 * T_ATT, KW),
            v(ROWS_ATT, 16 * T_ATT),
            v(ROWS_ATT, 16 * T_ATT),
            v(16 * T_ATT, LAT, dtype=F32),
            v(16 * T_ATT, LAT),
            v(CHIPS * T_ATT, LAT),
            v(CHIPS, T_ATT, LAT),
            v(8, CHIPS, 16, 256),
            v(CHIPS, 16, 256),
            v(CHIPS - 1, 16, 256),
            v(16, 256),
            v(N_EXP, 16, 256),
            dma((12 + len(COLS[0]),)),
            dma((4,)),
            dma((4,)),
            dma((2,)),
            dma((2,)),
            dma((3,)),
            dma((3,)),
            dma((36,)),
            dma((36,)),
            dma((8,)),
            dma((8,)),
            dma((10 * PIECES,)),
            dma((10 * PIECES,)),
            dma((PIECES,)),
            dma((PIECES,)),
            dma((10,)),
            dma((10,)),
        ],
        compiler_params=pltpu.CompilerParams(
            collective_id=0, has_side_effects=True, vmem_limit_bytes=58 * 1024 * 1024
        ),
        name="fused",
    )(ids, prio, docs, tok, grd, wg, wu, wd, lat, q, do)


def combine_kernel(ids_ref, prio_ref, gv_ref, back_ref, dq_in, dlat_in, dtok_ref, dg_ref, dq_ref, dlat_ref):
    ids = ids_ref[...]
    chosen, expert = route(ids, prio_ref[...])
    weight = jnp.zeros((PAIRS, 128), F32)
    for k in range(8):
        weight = weight + jnp.where(ids[k : k + 1, :] == expert, gv_ref[k : k + 1, :], 0.0)
    weight = weight * chosen
    w1 = weight.astype(BF).astype(F32)
    w2 = (weight - w1).astype(BF).astype(F32)
    w3 = weight - w1 - w2
    terms = jnp.concatenate([w3, w2, w1, jnp.zeros((PAIRS, 128), F32)], axis=0).T.astype(BF)
    for t in range(HALF // 512):
        rows = back_ref[:, :, pl.ds(EXTRA + t * 512, 512)].reshape(PAIRS, 512)
        stacked = jnp.concatenate([rows, rows, rows, rows], axis=0)
        dtok_ref[:, pl.ds(t * 512, 512)] = nn(terms, stacked).astype(BF)

    @pl.when(pl.program_id(0) == 0)
    def _():
        score = back_ref[:, :, pl.ds(0, EXTRA)].reshape(PAIRS, EXTRA).astype(F32)
        kept = chosen * score
        for k in range(8):
            own = jnp.where(ids[k : k + 1, :] == expert, kept, 0.0)
            dg_ref[k : k + 1, :] = jnp.sum(own, axis=0, keepdims=True).astype(BF)
        dq_ref[...] = dq_in[...]
        dlat_ref[...] = dlat_in[...]


def combine(ids, prio, gv, back, dq, dlat):
    def whole(shape):
        return pl.BlockSpec(shape, lambda h: (0,) * len(shape))

    return pl.pallas_call(
        combine_kernel,
        grid=(2,),
        out_shape=(
            jax.ShapeDtypeStruct((128, D), BF),
            jax.ShapeDtypeStruct((8, 128), BF),
            jax.ShapeDtypeStruct(dq.shape, BF),
            jax.ShapeDtypeStruct(dlat.shape, BF),
        ),
        in_specs=[
            whole((8, 128)),
            whole((1, 128)),
            whole((8, 128)),
            pl.BlockSpec((N_EXP, 2, OUTW), lambda h: (h, 0, 0)),
            whole(dq.shape),
            whole(dlat.shape),
        ],
        out_specs=(
            pl.BlockSpec((128, HALF), lambda h: (0, h)),
            whole((8, 128)),
            whole(dq.shape),
            whole(dlat.shape),
        ),
        name="combine",
    )(ids, prio, gv, back, dq, dlat)


def local(
    queries,
    latent,
    grad_out,
    doc_ids,
    tokens,
    token_grads,
    gate_values,
    expert_ids,
    gate_order,
    w_gate,
    w_up,
    w_down,
):
    ids = expert_ids.T
    back, dq, dlat = fused(
        ids,
        gate_order,
        doc_ids.reshape(1, T_ATT),
        tokens,
        token_grads,
        w_gate[0],
        w_up[0],
        w_down[0],
        latent,
        queries,
        grad_out,
    )
    d_tokens, d_gates, dq, dlat = combine(ids, gate_order, gate_values.T, back, dq, dlat)
    return (dq, dlat, d_tokens, d_gates.T)


def solution(mesh):
    in_specs = (
        P("ctx", "exp", None),
        P("ctx", None),
        P("ctx", "exp", None),
        P("ctx"),
        P(("ctx", "exp"), None),
        P(("ctx", "exp"), None),
        P(("ctx", "exp"), None),
        P(("ctx", "exp"), None),
        P(("ctx", "exp"), None),
        P("exp", None, "ctx"),
        P("exp", None, "ctx"),
        P("exp", "ctx", None),
    )
    out_specs = (
        P("ctx", "exp", None),
        P("ctx", None),
        P(("ctx", "exp"), None),
        P(("ctx", "exp"), None),
    )
    return jax.shard_map(local, mesh=mesh, in_specs=in_specs, out_specs=out_specs, check_vma=False)
```

```python
import jax
import jax.numpy as jnp
from jax import lax
from jax.experimental import pallas as pl
from jax.experimental.pallas import tpu as pltpu
from jax.sharding import PartitionSpec as P

SCALE = 192 ** (-0.5)
MESH = pl.DeviceIdType.MESH
BF = jnp.bfloat16
F32 = jnp.float32

N_X, N_CORE = 4, 2
N_EXP = 16
CHIPS = 8
D = 7168
HALF = D // 2
SHARD = 128
HID2 = 2 * SHARD
LAT = 512
KW = LAT + 128
T_ATT = 64
ROWS_ATT = 256
BLK = 64
PAIRS = 32
EXTRA = 128
OUTW = EXTRA + HALF
STEP = 256
HB = BLK // 2
OFFSETS = (0, 1, -1, 2, -2, 3, -3, 4, -4, 5, -5, 6, -6, 7, -7, 8)
COLS = (((0, OUTW),), ((0, 1152), (1152, 1024), (2176, 768), (2944, 768)))
PIECES = len(COLS[0]) + len(COLS[1])


def nt(a, b):
    return lax.dot_general(a, b, (((1,), (1,)), ((), ())), preferred_element_type=F32)


def nn(a, b):
    return lax.dot_general(a, b, (((1,), (0,)), ((), ())), preferred_element_type=F32)


def tn(a, b):
    return lax.dot_general(a, b, (((0,), (0,)), ((), ())), preferred_element_type=F32)


def route(ids, prio):
    pair = lax.broadcasted_iota(jnp.int32, (PAIRS, 128), 0)
    expert = lax.shift_right_logical(pair, 1)
    slot = (pair - 2 * expert).astype(F32)
    hits = jnp.zeros((PAIRS, 128), F32)
    for k in range(8):
        hits = hits + jnp.where(ids[k : k + 1, :] == expert, 1.0, 0.0)
    later = jnp.broadcast_to(prio.astype(F32), (128, 128))
    earlier = jnp.where(later.T < later, 1.0, 0.0)
    ranks = nn(hits.astype(BF), earlier.astype(BF))
    chosen = jnp.where((hits == 1.0) & (ranks == slot), 1.0, 0.0)
    return chosen, expert


def split_score(score):
    hi = score.astype(BF).astype(F32)
    lane = lax.broadcasted_iota(jnp.int32, (score.shape[0], EXTRA), 1)
    return jnp.where(lane == 0, hi, jnp.where(lane == 1, score - hi, 0.0)).astype(BF)


def kernel(
    ids_ref, prio_ref, docs_ref, tok_hbm, grd_hbm, wg_hbm, wu_hbm, wd_hbm, lat_hbm, q_hbm, do_hbm,
    back_ref, dq_ref, dlat_ref,
    rows_v, snd, ra, xg, wg, wu, wd, pbuf, prec, ggb, ugb, parts, rsx, rsd, rsm, s2p, s3p, rsf, rs2, ysend, rsy, bsend,
    q3, do3, qs, dos, qd, dqs, kbuf, dsb, pwb, dkf, dkb, drec, s2b, ebuf, e8, rbuf, f1, gbuf,
    sem_l, sem_as, sem_ar, sem_ks, sem_kr, sem_ws, sem_wr, sem_gs, sem_gr, sem_ps, sem_pr,
    sem_rs, sem_rr, sem_bs, sem_br, sem_ds, sem_dr,
):
    c = lax.axis_index("ctx")
    e = lax.axis_index("exp")
    core = lax.rem(c, 2)
    chip = lax.div(c, 2)
    y = lax.rem(chip, 2)
    x = lax.div(chip, 2)
    sib = c + 1 - 2 * core
    other = 1 - core
    right = 4 * lax.rem(x + 1, N_X) + 2 * y + core
    left = 4 * lax.rem(x + 3, N_X) + 2 * y + core
    mate = 4 * x + 2 * (1 - y) + core

    def at(ctx, exp):
        return {"ctx": ctx, "exp": exp}

    def remote(src, dst, ssem, rsem, ctx, exp):
        return pltpu.make_async_remote_copy(
            src_ref=src,
            dst_ref=dst,
            send_sem=ssem,
            recv_sem=rsem,
            device_id=at(ctx, exp),
            device_id_type=MESH,
        )

    def take(ref, sem):
        pltpu.make_async_copy(ref, ref, sem).wait()

    def entry(off, k):
        tc = lax.rem(core + k, 2)
        base = mate - core if off % 2 else 2 * chip
        return base + tc, tc

    def chip_at(r):
        return 2 * lax.rem(chip + r, CHIPS) + core

    lane0 = pl.multiple_of(core * SHARD, SHARD)
    own_d = pl.ds(pl.multiple_of(core * HALF, HALF), HALF)
    oth_d = pl.ds(pl.multiple_of(other * HALF, HALF), HALF)
    own_k = pl.ds(pl.multiple_of(core * 512, 512), 512)
    oth_k = pl.ds(pl.multiple_of(other * 512, 512), 512)
    own_b = pl.ds(pl.multiple_of(core * 512, 512), T_ATT)
    rows_in = [
        pltpu.make_async_copy(tok_hbm, rows_v.at[0], sem_l.at[0]),
        pltpu.make_async_copy(grd_hbm, rows_v.at[1], sem_l.at[1]),
    ]
    lat_in = pltpu.make_async_copy(lat_hbm, kbuf.at[own_b, pl.ds(0, LAT)], sem_l.at[2])
    att_in = [
        pltpu.make_async_copy(q_hbm, q3, sem_l.at[3]),
        pltpu.make_async_copy(do_hbm, do3, sem_l.at[4]),
    ]
    w_in = [
        pltpu.make_async_copy(wg_hbm.at[own_d, :], wg.at[:, pl.ds(lane0, SHARD)], sem_l.at[5]),
        pltpu.make_async_copy(wu_hbm.at[own_d, :], wu.at[:, pl.ds(lane0, SHARD)], sem_l.at[6]),
        pltpu.make_async_copy(wd_hbm.at[:, own_d], wd.at[pl.ds(lane0, SHARD), :], sem_l.at[7]),
    ]
    rows_in[0].start()
    lat_in.start()
    rows_in[1].start()

    bar = pltpu.get_barrier_semaphore()
    pl.semaphore_signal(bar, inc=1, device_id=at(sib, e), device_id_type=MESH)
    for r in range(1, CHIPS):
        pl.semaphore_signal(bar, inc=1, device_id=at(chip_at(r), e), device_id_type=MESH)
    for i in range(1, N_EXP):
        te = lax.rem(e + i, N_EXP)
        for k in range(N_CORE):
            pl.semaphore_signal(bar, inc=1, device_id=at(entry(i, k)[0], te), device_id_type=MESH)
        if i % 2:
            pl.semaphore_signal(bar, inc=1, device_id=at(c, te), device_id_type=MESH)
    for cp in att_in + w_in:
        cp.start()

    chosen, _ = route(ids_ref[...], prio_ref[...])
    picker = chosen.astype(BF)

    def pick(arr):
        rows_in[arr].wait()

        def body(t, carry):
            cols = pl.ds(pl.multiple_of(t * 512, 512), 512)
            val = nn(picker, rows_v[arr, :, cols]).astype(BF)
            snd[arr, :, :, cols] = val.reshape(N_EXP, 2, 512)
            return carry

        lax.fori_loop(0, D // 512, body, 0)

    def scatter(arr, b):
        for p in range(8):
            te = lax.rem(e + (N_EXP - OFFSETS[8 * b + p]) % N_EXP, N_EXP)
            for k in range(N_CORE):
                to, tc = entry(OFFSETS[8 * b + p], k)
                src = snd.at[arr, te, :, pl.ds(pl.multiple_of(tc * HALF, HALF), HALF)]
                dst = ra.at[arr, b, core * 8 + p]
                if b == 0 and p == 0 and k == 0:
                    pltpu.make_async_copy(src, dst, sem_l.at[8 + arr]).start()
                else:
                    sem = 2 * b + arr
                    remote(src, dst, sem_as.at[sem], sem_ar.at[sem], to, te).start()

    def incoming(buf, b):
        return buf.at[b, pl.ds(0, 15 + b)]

    pick(0)
    doc = lax.broadcasted_iota(jnp.int32, (128, T_ATT), 0)
    onehot_t = jnp.where(docs_ref[...] == doc, 1.0, 0.0).astype(BF)
    eye = jnp.where(
        lax.broadcasted_iota(jnp.int32, (128, 128), 0) == lax.broadcasted_iota(jnp.int32, (128, 128), 1),
        1.0,
        0.0,
    ).astype(BF)
    onehot = tn(onehot_t, eye).astype(BF)
    kbuf[own_b, pl.ds(LAT, 128)] = onehot
    lat_in.wait()

    pl.semaphore_wait(bar, 1 + 7 + 30 + 8)

    for r in range(1, CHIPS):
        row = core * 512 + (CHIPS - r) * T_ATT
        dst = kbuf.at[pl.ds(pl.multiple_of(row, T_ATT), T_ATT), :]
        remote(kbuf.at[own_b, :], dst, sem_ks.at[0], sem_kr.at[0], chip_at(r), e).start()
    scatter(0, 0)
    pick(1)
    scatter(1, 0)
    scatter(0, 1)
    scatter(1, 1)
    rem = [
        remote(wg_hbm.at[oth_d, :], wg.at[:, pl.ds(lane0, SHARD)], sem_ws.at[0], sem_wr.at[0], sib, e),
        remote(wu_hbm.at[oth_d, :], wu.at[:, pl.ds(lane0, SHARD)], sem_ws.at[1], sem_wr.at[1], sib, e),
        remote(wd_hbm.at[:, oth_d], wd.at[pl.ds(lane0, SHARD), :], sem_ws.at[2], sem_wr.at[2], sib, e),
    ]
    for cp in rem:
        cp.start()

    for cp in att_in:
        cp.wait()
    qs[...] = q3[...].reshape(ROWS_ATT, LAT)
    dos[...] = do3[...].reshape(ROWS_ATT, LAT)
    row_q = lax.shift_right_logical(lax.broadcasted_iota(jnp.int32, (ROWS_ATT, T_ATT), 0), 2)
    col_q = lax.broadcasted_iota(jnp.int32, (ROWS_ATT, T_ATT), 1)
    qd[...] = nn(jnp.where(row_q == col_q, 1.0, 0.0).astype(BF), onehot).astype(BF)

    hops = {}
    names = {}

    def hop(b, name, arr, dx, dy, way, lo=0, n=HB):
        if way == "R":
            to, tx, ty = right, (dx + 3) % 4, dy
        elif way == "L":
            to, tx, ty = left, (dx + 1) % 4, dy
        else:
            to, tx, ty = mate, dx, 1 - dy
        index = 18 * b + names.setdefault(name, len(names))
        hops[b, name] = remote(
            xg.at[arr, b, dx, pl.ds(dy * HB + lo, n), :],
            xg.at[arr, b, tx, pl.ds(ty * HB + lo, n), :],
            sem_gs.at[index],
            sem_gr.at[index],
            to,
            e,
        )
        hops[b, name].start()

    def got(b, *which):
        for name in which:
            hops[b, name].wait_recv()

    def repack(arr, b):
        if b == 0:
            pltpu.make_async_copy(
                snd.at[0, 0, :, pl.ds(0, HALF)], ra.at[arr, 0, 0], sem_l.at[8 + arr]
            ).wait()
        take(incoming(ra.at[arr], b), sem_ar.at[2 * b + arr])

        def body(t, carry):
            cols = pl.ds(pl.multiple_of(t * 512, 512), 512)
            xg[arr, b, 0, pl.ds(0, HB), cols] = ra[arr, b, :, :, cols].reshape(HB, 512)
            return carry

        lax.fori_loop(0, HALF // 512, body, 0)

    def hops_own(b):
        repack(0, b)
        hop(b, "TY", 0, 0, 0, "Y")
        hop(b, "TR", 0, 0, 0, "R")
        hop(b, "TL", 0, 0, 0, "L")
        repack(1, b)
        hop(b, "GR", 1, 0, 0, "R")
        hop(b, "GL", 1, 0, 0, "L")
        hop(b, "GY", 1, 0, 0, "Y")

    def hops_second(b):
        got(b, "TY")
        hop(b, "T1R", 0, 0, 1, "R")
        hop(b, "T1L", 0, 0, 1, "L")
        got(b, "GR", "GL")
        hop(b, "GlY", 1, 3, 0, "Y")
        hop(b, "GrY", 1, 1, 0, "Y")
        hop(b, "GhR", 1, 3, 0, "R", 0, HB // 2)
        hop(b, "GhL", 1, 1, 0, "L", HB // 2, HB // 2)
        got(b, "TR", "TL")
        hop(b, "ThR", 0, 3, 0, "R", 0, HB // 2)
        hop(b, "ThL", 0, 1, 0, "L", HB // 2, HB // 2)

    def hops_third(b):
        got(b, "GhR", "GhL")
        hop(b, "Gh0Y", 1, 2, 0, "Y", 0, HB // 2)
        hop(b, "Gh1Y", 1, 2, 0, "Y", HB // 2, HB // 2)
        got(b, "T1R", "T1L")
        hop(b, "T1hR", 0, 3, 1, "R", 0, HB // 2)
        hop(b, "T1hL", 0, 1, 1, "L", HB // 2, HB // 2)

    hops_own(0)
    take(kbuf.at[pl.ds(0, 7 * T_ATT), :], sem_kr.at[0])
    lat_sib = remote(kbuf.at[own_k, :], kbuf.at[own_k, :], sem_ks.at[1], sem_kr.at[1], sib, e)
    lat_sib.start()

    lat_sib.wait_recv()

    def att(h, carry):
        rows = pl.ds(pl.multiple_of(h * 64, 64), 64)
        keys = kbuf[:, :LAT]
        same = nt(qd[rows, :], kbuf[:, LAT:])
        s = nt(qs[rows, :], keys) * SCALE
        s = jnp.where(same > 0.5, s, -1e30)
        m = jnp.max(s, axis=1, keepdims=True)
        p = jnp.exp(s - m)
        total = jnp.sum(p, axis=1, keepdims=True)
        dp = nt(dos[rows, :], keys)
        delta = jnp.sum(p.astype(BF).astype(F32) * dp, axis=1, keepdims=True) / total
        probs = p / total
        ds = (probs * (dp - delta)).astype(BF)
        dsb[rows, :] = ds
        pwb[rows, :] = probs.astype(BF)
        dqs[rows, :] = (nn(ds, keys) * SCALE).astype(BF)
        return carry

    lax.fori_loop(0, ROWS_ATT // 64, att, 0)

    hops_second(0)

    def dkeys(k, carry):
        rows = pl.ds(pl.multiple_of(k * 128, 128), 128)
        val = tn(dsb[:, rows], qs[...]) * SCALE + tn(pwb[:, rows], dos[...])
        dkf[rows, :] = val
        dkb[rows, :] = val.astype(BF)
        return carry

    lax.fori_loop(0, CHIPS, dkeys, 0)
    dk_sib = remote(dkb.at[oth_k, :], drec, sem_ds.at[0], sem_dr.at[0], sib, e)
    dk_sib.start()

    for cp in w_in:
        cp.wait()
    for cp in rem:
        cp.wait_recv()

    swaps = {}

    def forward(b, dx):
        xt, xd = xg[0, b, dx], xg[1, b, dx]
        pbuf[b, dx, 0] = nn(xt, wg[...])
        pbuf[b, dx, 1] = nn(xt, wu[...])
        pbuf[b, dx, 2] = nt(xd, wd[...])
        index = 4 * b + dx
        swaps[b, dx] = remote(
            pbuf.at[b, dx], prec.at[b, dx], sem_ps.at[index], sem_pr.at[index], sib, e
        )
        swaps[b, dx].start()

    sends = {}

    def pass_on(kind, b, h, src, dst, to):
        index = PIECES * kind + len(COLS[0]) * b + h
        cols = pl.ds(*COLS[b][h])
        sends[kind, b, h] = remote(
            src.at[:, cols], dst.at[:, cols], sem_rs.at[index], sem_rr.at[index], to, e
        )
        sends[kind, b, h].start()

    def passed(kind, b, h):
        sends[kind, b, h].wait_recv()

    def wide(b, h):
        start, n = COLS[b][h]
        first = max(start - EXTRA, 0)
        return first, (start + n - EXTRA - first) // STEP

    def backward(b, dx, done):
        swaps[b, dx].wait_recv()
        gate = pbuf[b, dx, 0] + prec[b, dx, 0]
        up = pbuf[b, dx, 1] + prec[b, dx, 1]
        act = pbuf[b, dx, 2] + prec[b, dx, 2]
        sig = 1.0 / (1.0 + jnp.exp(-gate))
        silu = gate * sig
        hid = (silu * up).astype(BF).astype(F32)
        parts[b, dx, :, pl.ds(0, EXTRA)] = split_score(jnp.sum(hid * act, axis=1, keepdims=True))
        ggb[...] = (act * up * sig * (1.0 + gate * (1.0 - sig))).astype(BF)
        ugb[...] = (act * silu).astype(BF)
        for h in range(len(COLS[b])):
            first, steps = wide(b, h)

            def body(t, carry):
                at_col = first + t * STEP
                cols = pl.ds(pl.multiple_of(at_col, STEP), STEP)
                val = nt(ggb[...], wg[cols, :]) + nt(ugb[...], wu[cols, :])
                parts[b, dx, :, pl.ds(pl.multiple_of(EXTRA + at_col, 128), STEP)] = val.astype(BF)
                return carry

            lax.fori_loop(0, steps, body, 0)
            if done is not None:
                done(b, h)

    def merge(b, h, put, put_score, srcs):
        def summed(cols):
            val = srcs[0][:, cols].astype(F32)
            for ref in srcs[1:]:
                val = val + ref[:, cols].astype(F32)
            return val

        if h == 0:
            put_score(jnp.sum(summed(pl.ds(0, EXTRA)), axis=1, keepdims=True))
        first, steps = wide(b, h)

        def body(t, carry):
            cols = pl.ds(pl.multiple_of(EXTRA + first + t * STEP, 128), STEP)
            put(cols, summed(cols).astype(BF))
            return carry

        lax.fori_loop(0, steps, body, 0)

    def merge_into(b, h, dst, srcs):
        def put(cols, val):
            dst[:, cols] = val

        def put_score(score):
            dst[:, pl.ds(0, EXTRA)] = split_score(score)

        merge(b, h, put, put_score, srcs)

    mine, theirs = pl.ds(0, HB), pl.ds(HB, HB)
    lo, hi = pl.ds(0, HB // 2), pl.ds(HB // 2, HB // 2)

    def to_right(b, h):
        pass_on(0, b, h, parts.at[b, 1, theirs], rsx.at[b, 0], right)
        pass_on(8, b, h, parts.at[b, 1, hi], rsd.at[b, hi], right)

    def to_left(b, h):
        pass_on(1, b, h, parts.at[b, 3, theirs], rsx.at[b, 1], left)
        pass_on(9, b, h, parts.at[b, 3, lo], rsd.at[b, lo], left)

    def to_mate(b, h):
        pass_on(2, b, h, parts.at[b, 2, theirs], rsm.at[b], mate)

    def to_mate_sum(b, h):
        passed(0, b, h)
        passed(1, b, h)
        merge_into(b, h, ysend.at[b], [parts.at[b, 0, theirs], rsx.at[b, 0], rsx.at[b, 1]])
        pass_on(3, b, h, ysend.at[b], rsy.at[b], mate)

    def to_far(b, h):
        passed(2, b, h)
        merge_into(b, h, s2p.at[b], [parts.at[b, 2, mine], rsm.at[b]])
        pass_on(4, b, h, s2p.at[b, lo], rsf.at[b, 0], right)
        pass_on(5, b, h, s2p.at[b, hi], rsf.at[b, 1], left)

    def to_far_again(b, h):
        passed(4, b, h)
        merge_into(b, h, s3p.at[b, lo], [parts.at[b, 1, lo], rsf.at[b, 0]])
        pass_on(6, b, h, s3p.at[b, lo], rs2.at[b, lo], right)
        passed(5, b, h)
        merge_into(b, h, s3p.at[b, hi], [parts.at[b, 3, hi], rsf.at[b, 1]])
        pass_on(7, b, h, s3p.at[b, hi], rs2.at[b, hi], left)

    def give_back(b, h):
        def put(cols, val):
            bsend[b, :, :, cols] = val.reshape(16, 2, STEP)

        def put_score(score):
            val = jnp.broadcast_to(score, (HB, EXTRA)).astype(BF)
            bsend[b, :, :, pl.ds(0, EXTRA)] = val.reshape(16, 2, EXTRA)

        passed(8, b, h)
        passed(9, b, h)
        passed(3, b, h)
        passed(6, b, h)
        passed(7, b, h)
        merge(
            b,
            h,
            put,
            put_score,
            [parts.at[b, 0, mine], rsd.at[b], rsy.at[b], rs2.at[b]],
        )
        cols = pl.ds(*COLS[b][h])
        for p in range(8):
            te = lax.rem(e + OFFSETS[8 * b + p] % N_EXP, N_EXP)
            for k in range(N_CORE):
                to, tc = entry(OFFSETS[8 * b + p], k)
                src = bsend.at[b, tc * 8 + p, :, cols]
                dst = back_ref.at[core * N_EXP + e, :, cols]
                if b == 0 and p == 0 and k == 0:
                    pltpu.make_async_copy(src, dst, sem_l.at[12 + h]).start()
                else:
                    sem = len(COLS[0]) * b + h
                    remote(src, dst, sem_bs.at[sem], sem_br.at[sem], to, te).start()

    got(0, "GY")
    forward(0, 0)
    hops_own(1)
    hops_third(0)

    dk_sib.wait_recv()
    s2b[...] = (dkf[own_k, :] + drec[...].astype(F32)).astype(BF).reshape(CHIPS, T_ATT, LAT)

    def piece(z):
        return (
            pl.ds(pl.multiple_of(lax.div(z, 2) * 16, 16), 16),
            pl.ds(pl.multiple_of(lax.rem(z, 2) * 256, 256), 256),
        )

    rows_e, lanes_e = piece(lax.div(e, 2))
    own_piece = pltpu.make_async_copy(s2b.at[:, rows_e, lanes_e], ebuf.at[7], sem_l.at[10])
    own_piece.start()
    for i in range(1, 8):
        te = lax.rem(e + 2 * i, N_EXP)
        rows_t, lanes_t = piece(lax.div(te, 2))
        remote(s2b.at[:, rows_t, lanes_t], ebuf.at[i - 1], sem_ds.at[8], sem_dr.at[8], c, te).start()

    got(0, "GlY")
    forward(0, 3)
    got(0, "GrY")
    forward(0, 1)
    backward(0, 3, to_left)
    backward(0, 1, to_right)
    hops_second(1)
    got(0, "ThR", "ThL", "T1hR", "T1hL", "Gh0Y", "Gh1Y")
    forward(0, 2)
    backward(0, 0, None)
    backward(0, 2, to_mate)
    got(1, "GY")
    forward(1, 0)
    hops_third(1)
    for h in range(len(COLS[0])):
        to_mate_sum(0, h)
    for h in range(len(COLS[0])):
        to_far(0, h)
    got(1, "GlY")
    forward(1, 3)
    got(1, "GrY")
    forward(1, 1)
    backward(1, 3, to_left)
    backward(1, 1, to_right)
    for h in range(len(COLS[0])):
        to_far_again(0, h)

    own_piece.wait()
    take(ebuf.at[pl.ds(0, 7)], sem_dr.at[8])
    tot = ebuf[0].astype(F32)
    for i in range(1, 8):
        tot = tot + ebuf[i].astype(F32)
    e8[...] = tot.astype(BF)
    for r in range(1, CHIPS):
        remote(e8.at[r], rbuf.at[CHIPS - 1 - r], sem_ds.at[1], sem_dr.at[1], chip_at(r), e).start()
    dq_ref[...] = dqs[...].reshape(T_ATT, 4, LAT)
    got(1, "ThR", "ThL", "T1hR", "T1hL", "Gh0Y", "Gh1Y")
    forward(1, 2)
    backward(1, 2, to_mate)
    backward(1, 0, None)
    for h in range(len(COLS[0])):
        give_back(0, h)
    for h in range(len(COLS[1])):
        to_far(1, h)
    for h in range(len(COLS[1])):
        to_mate_sum(1, h)

    take(rbuf, sem_dr.at[1])
    tot = e8[0].astype(F32)
    for r in range(CHIPS - 1):
        tot = tot + rbuf[r].astype(F32)
    f1[...] = tot.astype(BF)
    own_final = pltpu.make_async_copy(f1, gbuf.at[e], sem_l.at[11])
    own_final.start()
    for i in range(1, N_EXP):
        te = lax.rem(e + i, N_EXP)
        remote(f1, gbuf.at[e], sem_ds.at[9], sem_dr.at[9], c, te).start()
    for h in range(len(COLS[1])):
        to_far_again(1, h)


    for h in range(len(COLS[1])):
        give_back(1, h)

    own_final.wait()
    take(gbuf.at[pl.ds(0, 15)], sem_dr.at[9])
    for z in range(8):
        both = gbuf[2 * z].astype(F32) + gbuf[2 * z + 1].astype(F32)
        dlat_ref[pl.ds(z // 2 * 16, 16), pl.ds(z % 2 * 256, 256)] = both.astype(BF)

    for b in range(2):
        for arr in range(2):
            take(incoming(ra.at[arr], b), sem_as.at[2 * b + arr])
    take(kbuf.at[pl.ds(0, 7 * T_ATT), :], sem_ks.at[0])
    lat_sib.wait_send()
    for cp in rem:
        cp.wait_send()
    for cp in hops.values():
        cp.wait_send()
    for cp in swaps.values():
        cp.wait_send()
    for cp in sends.values():
        cp.wait_send()
    dk_sib.wait_send()
    take(ebuf.at[pl.ds(0, 7)], sem_ds.at[8])
    take(rbuf, sem_ds.at[1])
    take(gbuf.at[pl.ds(0, 15)], sem_ds.at[9])
    for b in range(2):
        for h, (start, n) in enumerate(COLS[b]):
            cols = pl.ds(start, n)
            if b == 0:
                own = bsend.at[0, 0, :, cols], back_ref.at[0, :, cols]
                pltpu.make_async_copy(*own, sem_l.at[12 + h]).wait()
            for sems in (sem_bs, sem_br):
                take(bsend.at[b, pl.ds(0, 15 + b), :, cols], sems.at[len(COLS[0]) * b + h])


def fused(ids, prio, docs, tok, grd, wg, wu, wd, lat, q, do):
    vmem = pl.BlockSpec(memory_space=pltpu.VMEM)
    hbm = pl.BlockSpec(memory_space=pl.ANY)
    dma = pltpu.SemaphoreType.DMA

    def v(*shape, dtype=BF):
        return pltpu.VMEM(shape, dtype)

    return pl.pallas_call(
        kernel,
        out_shape=(
            jax.ShapeDtypeStruct((PAIRS, 2, OUTW), BF),
            jax.ShapeDtypeStruct((T_ATT, 4, LAT), BF),
            jax.ShapeDtypeStruct((T_ATT, LAT), BF),
        ),
        in_specs=[vmem] * 3 + [hbm] * 8,
        out_specs=(vmem, vmem, vmem),
        scratch_shapes=[
            v(2, 128, D),
            v(2, N_EXP, 2, D),
            v(2, 2, 16, 2, HALF),
            v(2, 2, N_X, 2 * HB, HALF),
            v(HALF, HID2),
            v(HALF, HID2),
            v(HID2, HALF),
            v(2, N_X, 3, 2 * HB, HID2, dtype=F32),
            v(2, N_X, 3, 2 * HB, HID2, dtype=F32),
            v(2 * HB, HID2),
            v(2 * HB, HID2),
            v(2, N_X, 2 * HB, OUTW),
            v(2, 2, HB, OUTW),
            v(2, HB, OUTW),
            v(2, HB, OUTW),
            v(2, HB, OUTW),
            v(2, HB, OUTW),
            v(2, 2, HB // 2, OUTW),
            v(2, HB, OUTW),
            v(2, HB, OUTW),
            v(2, HB, OUTW),
            v(2, 16, 2, OUTW),
            v(T_ATT, 4, LAT),
            v(T_ATT, 4, LAT),
            v(ROWS_ATT, LAT),
            v(ROWS_ATT, LAT),
            v(ROWS_ATT, 128),
            v(ROWS_ATT, LAT),
            v(16 * T_ATT, KW),
            v(ROWS_ATT, 16 * T_ATT),
            v(ROWS_ATT, 16 * T_ATT),
            v(16 * T_ATT, LAT, dtype=F32),
            v(16 * T_ATT, LAT),
            v(CHIPS * T_ATT, LAT),
            v(CHIPS, T_ATT, LAT),
            v(8, CHIPS, 16, 256),
            v(CHIPS, 16, 256),
            v(CHIPS - 1, 16, 256),
            v(16, 256),
            v(N_EXP, 16, 256),
            dma((12 + len(COLS[0]),)),
            dma((4,)),
            dma((4,)),
            dma((2,)),
            dma((2,)),
            dma((3,)),
            dma((3,)),
            dma((36,)),
            dma((36,)),
            dma((8,)),
            dma((8,)),
            dma((10 * PIECES,)),
            dma((10 * PIECES,)),
            dma((PIECES,)),
            dma((PIECES,)),
            dma((10,)),
            dma((10,)),
        ],
        compiler_params=pltpu.CompilerParams(
            collective_id=0, has_side_effects=True, vmem_limit_bytes=58 * 1024 * 1024
        ),
        name="fused",
    )(ids, prio, docs, tok, grd, wg, wu, wd, lat, q, do)


def combine_kernel(ids_ref, prio_ref, gv_ref, back_ref, dq_in, dlat_in, dtok_ref, dg_ref, dq_ref, dlat_ref):
    ids = ids_ref[...]
    chosen, expert = route(ids, prio_ref[...])
    weight = jnp.zeros((PAIRS, 128), F32)
    for k in range(8):
        weight = weight + jnp.where(ids[k : k + 1, :] == expert, gv_ref[k : k + 1, :], 0.0)
    weight = weight * chosen
    w1 = weight.astype(BF).astype(F32)
    w2 = (weight - w1).astype(BF).astype(F32)
    w3 = weight - w1 - w2
    terms = jnp.concatenate([w3, w2, w1, jnp.zeros((PAIRS, 128), F32)], axis=0).T.astype(BF)
    for t in range(HALF // 512):
        rows = back_ref[:, :, pl.ds(EXTRA + t * 512, 512)].reshape(PAIRS, 512)
        stacked = jnp.concatenate([rows, rows, rows, rows], axis=0)
        dtok_ref[:, pl.ds(t * 512, 512)] = nn(terms, stacked).astype(BF)

    @pl.when(pl.program_id(0) == 0)
    def _():
        score = back_ref[:, :, pl.ds(0, EXTRA)].reshape(PAIRS, EXTRA).astype(F32)
        kept = chosen * score
        for k in range(8):
            own = jnp.where(ids[k : k + 1, :] == expert, kept, 0.0)
            dg_ref[k : k + 1, :] = jnp.sum(own, axis=0, keepdims=True).astype(BF)
        dq_ref[...] = dq_in[...]
        dlat_ref[...] = dlat_in[...]


def combine(ids, prio, gv, back, dq, dlat):
    def whole(shape):
        return pl.BlockSpec(shape, lambda h: (0,) * len(shape))

    return pl.pallas_call(
        combine_kernel,
        grid=(2,),
        out_shape=(
            jax.ShapeDtypeStruct((128, D), BF),
            jax.ShapeDtypeStruct((8, 128), BF),
            jax.ShapeDtypeStruct(dq.shape, BF),
            jax.ShapeDtypeStruct(dlat.shape, BF),
        ),
        in_specs=[
            whole((8, 128)),
            whole((1, 128)),
            whole((8, 128)),
            pl.BlockSpec((N_EXP, 2, OUTW), lambda h: (h, 0, 0)),
            whole(dq.shape),
            whole(dlat.shape),
        ],
        out_specs=(
            pl.BlockSpec((128, HALF), lambda h: (0, h)),
            whole((8, 128)),
            whole(dq.shape),
            whole(dlat.shape),
        ),
        name="combine",
    )(ids, prio, gv, back, dq, dlat)


def local(
    queries,
    latent,
    grad_out,
    doc_ids,
    tokens,
    token_grads,
    gate_values,
    expert_ids,
    gate_order,
    w_gate,
    w_up,
    w_down,
):
    ids = expert_ids.T
    back, dq, dlat = fused(
        ids,
        gate_order,
        doc_ids.reshape(1, T_ATT),
        tokens,
        token_grads,
        w_gate[0],
        w_up[0],
        w_down[0],
        latent,
        queries,
        grad_out,
    )
    d_tokens, d_gates, dq, dlat = combine(ids, gate_order, gate_values.T, back, dq, dlat)
    return (dq, dlat, d_tokens, d_gates.T)


def solution(mesh):
    in_specs = (
        P("ctx", "exp", None),
        P("ctx", None),
        P("ctx", "exp", None),
        P("ctx"),
        P(("ctx", "exp"), None),
        P(("ctx", "exp"), None),
        P(("ctx", "exp"), None),
        P(("ctx", "exp"), None),
        P(("ctx", "exp"), None),
        P("exp", None, "ctx"),
        P("exp", None, "ctx"),
        P("exp", "ctx", None),
    )
    out_specs = (
        P("ctx", "exp", None),
        P("ctx", None),
        P(("ctx", "exp"), None),
        P(("ctx", "exp"), None),
    )
    return jax.shard_map(local, mesh=mesh, in_specs=in_specs, out_specs=out_specs, check_vma=False)
```
